256 devices in a mesh: tensor: 32 (over z, x), adapter: 8 (over y, core).
Axes of the slice: x: 4, y: 4, z: 8, core: 2. Of those that a mesh axis runs over, the one named last changes fastest.
Arguments:
- tokens: bfloat16 [4096, 2880], P(('adapter', 'tensor')), may hold values from -6 to 6
- gain_attention: float32 [2880], replicated, may hold values from 0.1 to 1.9
- query_weight: bfloat16 [2880, 4096], P(None, 'tensor'), may hold values from -0.109375 to 0.109375
- keyval_weight: bfloat16 [2880, 2, 64, 8], P(None, None, 'tensor'), may hold values from -0.109375 to 0.109375
- output_weight: bfloat16 [4096, 2880], P('tensor'), may hold values from -0.09375 to 0.09375
- sink_logits: float32 [64], P('tensor'), may hold values from -1 to 2
- heads_down: bfloat16 [64, 48, 2880], P('adapter'), may hold values from -0.109375 to 0.109375
- query_up: bfloat16 [64, 16, 4096], P(None, None, 'tensor'), may hold values from -1.5 to 1.5
- keyval_up: bfloat16 [64, 2, 16, 64, 8], P(None, None, None, 'tensor'), may hold values from -1.5 to 1.5
- output_down: bfloat16 [64, 16, 4096], P(None, None, 'tensor'), may hold values from -0.09375 to 0.09375
- output_up: bfloat16 [64, 16, 2880], P('tensor'), may hold values from -1.5 to 1.5
- gain_mixture: float32 [2880], replicated, may hold values from 0.1 to 1.9
- gate_up_weight: bfloat16 [2880, 2, 11520], P(None, None, 'tensor'), may hold values from -0.109375 to 0.109375
- down_weight: bfloat16 [11520, 2880], P('tensor'), may hold values from -0.109375 to 0.109375
- mixture_down: bfloat16 [64, 16, 2880], P('adapter'), may hold values from -0.109375 to 0.109375
- mixture_up: bfloat16 [64, 16, 2880], P('tensor'), may hold values from -1.5 to 1.5
- lengths: int32 [8, 8], replicated, may hold values from 1 to 256, 512 in all within a row
- prompt_adapter: int32 [8, 8], replicated, may hold values from 0 to 63
- adapter_slot: int32 [64], replicated, may hold values from 0 to 63, each once
- expert_ids: int32 [4096, 4], P('adapter'), may hold values from 0 to 31, all different within a row; in each aligned block of 512 rows (0 to 511, 512 to 1023, ...) at most 128 rows name the same one
- expert_weights: float32 [4096, 4], P('adapter'), may hold values from 0.05 to 0.5
Outputs:
- layer_out: bfloat16 [4096, 2880], P(('adapter', 'tensor'))
The draws below stay inside these ranges and needn't reach their ends.
Inputs may be any that keep to these rules, and one draw needn't show every extreme that they name: `expert_ids`: in each group of 512 tokens no expert is named by more than 128 tokens.
All inputs are finite; a program needn't handle non-finite values.
Results may differ from the reference program's by a relative error of at most 0.02.
Values may be sent and summed in bfloat16 or wider, within the bound.
A program may use at most 128 MiB of HBM per device.

```python
import math
import jax
import jax.numpy as jnp
import numpy as np
from jax import lax

D = 2880
QH = 64
KVH = 8
HD = 64
FF = 2880
WINDOW = 128
TOP = 4
ROUTED = 32
EXPERTS = 4
R = 16
ACTIVE = 16
PROMPTS = 8
TOK_DEV = 16
GROUP = 512
TOKENS = 4096
ADAPTERS = 64
LONGEST = 256
CAP = 128
N_TENSOR = 32
N_ADAPTER = 8


def draw_prompt_adapter(key, part):
    pick_key, first_key, second_key = jax.random.split(key, 3)
    chosen = jax.random.permutation(pick_key, ADAPTERS)[:ACTIVE]
    first_pick = jax.random.randint(first_key, (N_ADAPTER, PROMPTS), 0, ACTIVE)
    second_pick = jax.random.randint(second_key, (N_ADAPTER, PROMPTS), 0, ACTIVE)
    return chosen[jnp.minimum(first_pick, second_pick)].astype(jnp.int32)


def shard_levels(stream_key, dims, cuts, least, high):
    loudness, own = 1.0, jax.random.fold_in(stream_key, 6)
    for axis_at, parts in cuts:
        steps = jnp.exp(jax.random.uniform(jax.random.fold_in(own, axis_at), (parts,), jnp.float32, least / len(cuts), high / len(cuts)))
        loudness = loudness * jnp.repeat(steps, dims[axis_at] // parts).reshape([-1 if axis == axis_at else 1 for axis in range(len(dims))])
    return loudness


def profile(number_of, total, bound, slope):
    weights = [(1 << 20) // math.isqrt(grade ** slope) + 1 for grade in range(2, number_of + 1)]
    rest, counts = total - bound - (number_of - 1), [1] * (number_of - 1)
    while rest > 0:
        movable = [i for i in range(number_of - 1) if counts[i] < bound]
        whole, budget = sum([weights[i] for i in movable]), rest
        for i in movable:
            extra = min(bound - counts[i], max(1, budget * weights[i] // whole), rest)
            counts[i] = counts[i] + extra
            rest = rest - extra
    return np.array([bound] + counts)


def uneven(stream_key, amount, total, most, slope):
    if amount == 2:
        one = jax.random.randint(stream_key, (), max(1, total - most), min(most, total - 1) + 1)
        return jnp.stack([one, total - one])
    sizes = jnp.asarray(profile(amount, total, most, slope), jnp.int32)
    twos = (amount - 1) // 2
    source_of, receiver = sizes[1:1 + 2 * twos:2], sizes[2:2 + 2 * twos:2]
    slack = jnp.minimum(source_of - 1, most - receiver)
    shifted = jax.random.randint(jax.random.fold_in(stream_key, 1), (twos,), 0, 1 << 20) % (slack + 1)
    sizes = sizes.at[1:1 + 2 * twos:2].set(source_of - shifted).at[2:2 + 2 * twos:2].set(receiver + shifted)
    return sizes[jax.random.permutation(jax.random.fold_in(stream_key, 2), amount)]


def deal_out(own_key, own, number, rows, count, top, most, skew):
    ranking = jax.random.permutation(own_key, count)
    packed, usual = portions_of(count, rows * top, most, skew, True), portions_of(count, rows * top, most, skew, False)
    places = jnp.arange(count)

    def named(sizes, rotation):
        used = int((sizes > 0).sum())
        fixed = max(1, used // 4)
        passed = fixed + (places - fixed + rotation * (used - fixed)) % max(1, count - fixed)
        return jnp.zeros((count,), jnp.int32).at[ranking[jnp.where(places < fixed, places, passed)]].set(jnp.asarray(sizes, jnp.int32))

    sizes = jnp.where(number % 4 == 0, named(packed, number // 4), named(usual, number - number // 4 - 1))
    mixed = jax.random.permutation(jax.random.fold_in(own, 3), count)
    giver, taker = mixed[0:count // 2 * 2:2], mixed[1:count // 2 * 2:2]
    room = jnp.minimum(sizes[giver] - 1, most - sizes[taker]) // 2
    room = jnp.where((giver == ranking[0]) | (taker == ranking[0]) | (sizes[taker] == 0), 0, jnp.maximum(room, 0))
    passed = jax.random.randint(jax.random.fold_in(own, 4), (count // 2,), 0, 1 << 20) % (room + 1)
    sizes = sizes.at[giver].add(-passed).at[taker].add(passed)
    items = jnp.searchsorted(jnp.cumsum(sizes), jnp.arange(rows * top), side="right").astype(jnp.int32)
    table = items.reshape(top, rows).T
    table = table[jax.random.permutation(jax.random.fold_in(own, 1), rows)]
    rotation = jax.random.randint(jax.random.fold_in(own, 2), (rows, 1), 0, top)
    return jnp.take_along_axis(table, (jnp.arange(top)[None, :] + rotation) % top, axis=1)


def portions_of(number_of, total, bound, lean, full):
    portions = [(1 << 20) // math.isqrt(grade ** lean) + 1 for grade in range(1, number_of + 1)]
    largest = bound if full else min(bound, max(-(-total // number_of), total * portions[0] // sum(portions)))
    least = 1 if total - largest >= number_of - 1 else 0
    counts, rest = [largest] + [least] * (number_of - 1), total - largest - least * (number_of - 1)
    while rest > 0:
        free = [i for i in range(1, number_of) if counts[i] < largest] or [i for i in range(1, number_of) if counts[i] < bound]
        pool, budget = sum([portions[i] for i in free]), rest
        for i in free:
            extra = min(bound - counts[i], max(1, budget * portions[i] // pool), rest)
            counts[i] = counts[i] + extra
            rest = rest - extra
    return np.array(counts)


def noise(rng, shape, deviation, limit, cuts=(), kind=jnp.bfloat16):
    entries = deviation * jax.random.normal(rng, shape, jnp.float32)
    if cuts:
        entries = entries * shard_levels(rng, shape, cuts, -0.22, 0.18)
    return jnp.clip(entries, -limit, limit).astype(kind)


def setup_inputs(seed: int = 0) -> dict:
    keys = jax.random.split(jax.random.key(seed), 22)
    tokens = noise(keys[0], (TOKENS, D), 1.0, 6.0, ((0, 256),))
    gain_attention = jnp.clip(1.0 + 0.18 * jax.random.normal(keys[1], (D,), jnp.float32), 0.1, 1.9)
    query_weight = noise(keys[2], (D, QH * HD), D ** -0.5, 0.109375, ((1, 32),))
    keyval_weight = noise(keys[3], (D, 2, HD, KVH), D ** -0.5, 0.109375, ((2, 32),))
    output_weight = noise(keys[4], (QH * HD, D), (QH * HD) ** -0.5, 0.09375, ((0, 32),))
    sink_logits = jnp.clip(-1.0 + 3.0 * jax.random.uniform(keys[5], (QH,), jnp.float32) ** shard_levels(keys[5], (QH,), ((0, 32),), -0.2, 0.2), -1.0, 2.0)
    heads_down = noise(keys[6], (ADAPTERS, 3 * R, D), D ** -0.5, 0.109375, ((0, 8),))
    query_up = noise(keys[7], (ADAPTERS, R, QH * HD), R ** -0.5, 1.5, ((2, 32),))
    keyval_up = noise(keys[8], (ADAPTERS, 2, R, HD, KVH), R ** -0.5, 1.5, ((3, 32),))
    output_down = noise(keys[9], (ADAPTERS, R, QH * HD), (QH * HD) ** -0.5, 0.09375, ((2, 32),))
    output_up = noise(keys[10], (ADAPTERS, R, D), R ** -0.5, 1.5, ((0, 32),))
    gain_mixture = jnp.clip(1.0 + 0.18 * jax.random.normal(keys[11], (D,), jnp.float32), 0.1, 1.9)
    gate_up_weight = noise(keys[12], (D, 2, EXPERTS * FF), D ** -0.5, 0.109375, ((2, 32),))
    down_weight = noise(keys[13], (EXPERTS * FF, D), FF ** -0.5, 0.109375, ((0, 32),))
    mixture_down = noise(keys[14], (ADAPTERS, R, D), D ** -0.5, 0.109375, ((0, 8),))
    mixture_up = noise(keys[15], (ADAPTERS, R, D), R ** -0.5, 1.5, ((0, 32),))
    lengths = jax.vmap(lambda own: uneven(own, PROMPTS, GROUP, LONGEST, 2))(jax.random.split(keys[16], N_ADAPTER)).reshape((N_ADAPTER, PROMPTS)).astype(jnp.int32)
    prompt_adapter = draw_prompt_adapter(jax.random.fold_in(keys[21], 71), 0)
    adapter_slot = jax.random.permutation(keys[18], ADAPTERS).astype(jnp.int32)
    expert_ids_keys = jax.random.split(jax.random.fold_in(keys[19], 1), TOKENS // GROUP)
    expert_ids_turns = jax.random.permutation(jax.random.fold_in(keys[19], 3), TOKENS // GROUP)
    expert_ids = jax.vmap(lambda own, number: deal_out(jax.random.fold_in(keys[19], 2), own, number, GROUP, ROUTED, TOP, CAP, 1))(expert_ids_keys, expert_ids_turns).reshape((TOKENS, TOP))
    expert_weights = jnp.clip(0.05 + 0.45 * jax.random.uniform(keys[20], (TOKENS, TOP), jnp.float32) ** shard_levels(keys[20], (TOKENS, TOP), ((0, 8),), -0.2, 0.2), 0.05, 0.5)
    return dict(tokens=tokens, gain_attention=gain_attention, query_weight=query_weight, keyval_weight=keyval_weight, output_weight=output_weight, sink_logits=sink_logits, heads_down=heads_down, query_up=query_up, keyval_up=keyval_up, output_down=output_down, output_up=output_up, gain_mixture=gain_mixture, gate_up_weight=gate_up_weight, down_weight=down_weight, mixture_down=mixture_down, mixture_up=mixture_up, lengths=lengths, prompt_adapter=prompt_adapter, adapter_slot=adapter_slot, expert_ids=expert_ids, expert_weights=expert_weights)


NORM_EPS = 1e-05
ROPE_BASE = 150000.0
SWIGLU_ALPHA = 1.702

def token_tables(length_row, adapter_row, first_row, row_count):
    prompt_ends = jnp.cumsum(length_row).astype(jnp.int32)
    prompt_starts = (prompt_ends - length_row).astype(jnp.int32)
    token_index = first_row + jnp.arange(row_count, dtype=jnp.int32)
    member = (token_index[:, None] >= prompt_starts[None, :]) & (token_index[:, None] < prompt_ends[None, :])
    prompt_index = jnp.arange(length_row.shape[0], dtype=jnp.int32)
    segment = lax.optimization_barrier(jnp.sum(jnp.where(member, prompt_index[None, :], 0), axis=1)).astype(jnp.int32)
    prompt_begin = lax.optimization_barrier(jnp.sum(jnp.where(member, prompt_starts[None, :], 0), axis=1)).astype(jnp.int32)
    adapter = lax.optimization_barrier(jnp.sum(jnp.where(member, adapter_row[None, :], 0), axis=1)).astype(jnp.int32)
    return (segment, (token_index - prompt_begin).astype(jnp.int32), adapter)

def settle(values):
    return lax.optimization_barrier(values.astype(jnp.bfloat16)).astype(jnp.float32)

def rms_scale(row_block, gain):
    wide = row_block.astype(jnp.float32)
    mean_square = lax.optimization_barrier(jnp.mean(wide * wide, axis=-1, keepdims=True))
    return (wide * lax.rsqrt(mean_square + NORM_EPS) * gain).astype(jnp.bfloat16)

def rotate(head_rows, position):
    half_width = head_rows.shape[-1] // 2
    freqs = jnp.exp(-math.log(ROPE_BASE) * jnp.arange(half_width, dtype=jnp.float32) / half_width)
    angles = position.astype(jnp.float32)[:, None] * freqs[None, :]
    cosine = jnp.cos(angles)[:, None, :]
    sine_val = jnp.sin(angles)[:, None, :]
    first_half = head_rows[..., :half_width]
    second_half = head_rows[..., half_width:]
    return jnp.concatenate([first_half * cosine - second_half * sine_val, second_half * cosine + first_half * sine_val], axis=-1)

def spread_rank(onehot, rank_rows):
    return (onehot[:, :, None] * rank_rows[:, None, :]).reshape(rank_rows.shape[0], -1)

def down_rank(normed, bank, slot_hot):
    row_count = normed.shape[0]
    stored, rank_width, width_d = bank.shape
    projected = jnp.dot(normed, bank.reshape(stored * rank_width, width_d).T, preferred_element_type=jnp.float32)
    projected = projected.reshape(row_count, stored, rank_width)
    return lax.optimization_barrier(jnp.sum(projected * slot_hot[:, :, None], axis=1)).astype(jnp.bfloat16)

def attend(queries, key_rows, value_rows, segment, sink_logits):
    row_count = queries.shape[0]
    block_rows = min(512, row_count)
    key_pad = jnp.pad(key_rows, ((WINDOW, 0), (0, 0), (0, 0)))
    value_pad = jnp.pad(value_rows, ((WINDOW, 0), (0, 0), (0, 0)))
    segment_pad = jnp.pad(segment, (WINDOW, 0), constant_values=-1)
    sink_weight = jnp.exp(sink_logits.astype(jnp.float32))[:, None]
    score_scale = queries.shape[-1] ** (-0.5)

    def one_block(block_start):
        query_block = lax.dynamic_slice_in_dim(queries, block_start, block_rows, 0).astype(jnp.float32)
        key_block = lax.dynamic_slice_in_dim(key_pad, block_start, block_rows + WINDOW, 0).astype(jnp.float32)
        value_block = lax.dynamic_slice_in_dim(value_pad, block_start, block_rows + WINDOW, 0).astype(jnp.float32)
        segment_query = lax.dynamic_slice_in_dim(segment, block_start, block_rows, 0)
        segment_key = lax.dynamic_slice_in_dim(segment_pad, block_start, block_rows + WINDOW, 0)
        row_pos = jnp.arange(block_rows, dtype=jnp.int32)[:, None] + WINDOW
        col_pos = jnp.arange(block_rows + WINDOW, dtype=jnp.int32)[None, :]
        allowed = (segment_query[:, None] == segment_key[None, :]) & (col_pos <= row_pos) & (row_pos - col_pos < WINDOW)
        scores = jnp.einsum('qhd,khd->hqk', query_block, key_block) * score_scale
        weights = jnp.where(allowed[None], jnp.exp(scores), 0.0)
        denominator = sink_weight + lax.optimization_barrier(jnp.sum(weights, axis=-1))
        weights_bf = (weights / denominator[..., None]).astype(jnp.bfloat16)
        mixed_block = jnp.einsum('hqk,khd->qhd', weights_bf.astype(jnp.float32), value_block)
        return mixed_block.astype(jnp.bfloat16).reshape(block_rows, -1)
    block_starts = jnp.arange(row_count // block_rows, dtype=jnp.int32) * block_rows
    return lax.map(one_block, block_starts).reshape(row_count, -1)

def reference(tokens, gain_attention, query_weight, keyval_weight, output_weight, sink_logits, heads_down, query_up, keyval_up, output_down, output_up, gain_mixture, gate_up_weight, down_weight, mixture_down, mixture_up, lengths, prompt_adapter, adapter_slot, expert_ids, expert_weights):
    group_rows = TOK_DEV * N_TENSOR
    adapter_count = adapter_slot.shape[0]
    query_cols = QH * HD // N_TENSOR
    local_count = adapter_count // N_TENSOR
    slice_width = EXPERTS * FF // N_TENSOR
    adapter_ids = jnp.arange(adapter_count, dtype=jnp.int32)
    block_ids = jnp.arange(N_TENSOR, dtype=jnp.int32)
    gate_all = gate_up_weight[:, 0]
    lift_all = gate_up_weight[:, 1]
    key_weight = jnp.transpose(keyval_weight[:, 0], (0, 2, 1)).reshape(D, KVH * HD)
    value_weight = jnp.transpose(keyval_weight[:, 1], (0, 2, 1)).reshape(D, KVH * HD)
    key_up = jnp.transpose(keyval_up[:, 0], (0, 1, 3, 2)).reshape(adapter_count * R, KVH * HD)
    value_up = jnp.transpose(keyval_up[:, 1], (0, 1, 3, 2)).reshape(adapter_count * R, KVH * HD)

    def one_group(inputs):
        token_rows, length_row, adapter_row, id_rows, weight_rows = inputs
        segment, position, adapter = token_tables(length_row, adapter_row, jnp.int32(0), group_rows)
        adapter_hit = adapter[:, None] == adapter_ids[None, :]
        onehot = adapter_hit.astype(jnp.bfloat16)
        onehot_wide = adapter_hit.astype(jnp.float32)
        slot_ids = lax.optimization_barrier(jnp.sum(jnp.where(adapter_hit, adapter_slot[None, :], 0), axis=1)).astype(jnp.int32)
        slot_hot = (slot_ids[:, None] == adapter_ids[None, :]).astype(jnp.float32)
        normed = rms_scale(token_rows, gain_attention)
        rank_qkv = down_rank(normed, heads_down, slot_hot)
        queries = jnp.dot(normed, query_weight, preferred_element_type=jnp.float32)
        queries = queries + jnp.dot(spread_rank(onehot, rank_qkv[:, :R]), query_up.reshape(adapter_count * R, QH * HD), preferred_element_type=jnp.float32)
        queries = rotate(queries.reshape(group_rows, QH, HD), position).astype(jnp.bfloat16)
        key_raw = jnp.dot(normed, key_weight, preferred_element_type=jnp.float32)
        key_raw = (key_raw + jnp.dot(spread_rank(onehot, rank_qkv[:, R:2 * R]), key_up, preferred_element_type=jnp.float32)).astype(jnp.bfloat16)
        value_rows = jnp.dot(normed, value_weight, preferred_element_type=jnp.float32)
        value_rows = (value_rows + jnp.dot(spread_rank(onehot, rank_qkv[:, 2 * R:3 * R]), value_up, preferred_element_type=jnp.float32)).astype(jnp.bfloat16)
        key_rows = rotate(key_raw.astype(jnp.float32).reshape(group_rows, KVH, HD), position).astype(jnp.bfloat16)
        repeat_count = QH // KVH
        mixed_rows = attend(queries, jnp.repeat(key_rows, repeat_count, axis=1), jnp.repeat(value_rows.reshape(group_rows, KVH, HD), repeat_count, axis=1), segment, sink_logits)

        def rank_block(carry, block_index):
            col_block = lax.dynamic_slice_in_dim(mixed_rows, block_index * query_cols, query_cols, 1)
            rank_table = lax.dynamic_slice_in_dim(output_down, block_index * query_cols, query_cols, 2).reshape(adapter_count * R, query_cols)
            terms = jnp.dot(col_block, rank_table.T, preferred_element_type=jnp.float32).reshape(group_rows, adapter_count, R)
            return (carry + settle(lax.optimization_barrier(jnp.sum(terms * onehot_wide[:, :, None], axis=1))), None)
        rank_sum, _ = lax.scan(rank_block, jnp.zeros((group_rows, R), jnp.float32), block_ids)
        spread_out = spread_rank(onehot, rank_sum.astype(jnp.bfloat16))

        def attn_block(carry, block_index):
            col_block = lax.dynamic_slice_in_dim(mixed_rows, block_index * query_cols, query_cols, 1)
            weight_rows_o = lax.dynamic_slice_in_dim(output_weight, block_index * query_cols, query_cols, 0)
            spread_mine = lax.dynamic_slice_in_dim(spread_out, block_index * local_count * R, local_count * R, 1)
            up_rows = lax.dynamic_slice_in_dim(output_up, block_index * local_count, local_count, 0).reshape(local_count * R, D)
            term = jnp.dot(col_block, weight_rows_o, preferred_element_type=jnp.float32) + jnp.dot(spread_mine, up_rows, preferred_element_type=jnp.float32)
            return (carry + settle(term), None)
        attn_sum, _ = lax.scan(attn_block, jnp.zeros((group_rows, D), jnp.float32), block_ids)
        hidden = token_rows.astype(jnp.float32) + attn_sum
        normed_two = rms_scale(hidden, gain_mixture)
        rank_moe = down_rank(normed_two, mixture_down, slot_hot)
        spread_moe = spread_rank(onehot, rank_moe)

        def moe_block(carry, block_index):
            first_col = block_index * slice_width
            expert = first_col // FF
            route_weight = lax.optimization_barrier(jnp.sum(jnp.where(id_rows == expert, weight_rows, 0.0), axis=1))
            gate_val = jnp.dot(normed_two, lax.dynamic_slice_in_dim(gate_all, first_col, slice_width, 1), preferred_element_type=jnp.float32)
            lift_val = jnp.dot(normed_two, lax.dynamic_slice_in_dim(lift_all, first_col, slice_width, 1), preferred_element_type=jnp.float32)
            active = ((lift_val + 1.0) * gate_val * jax.nn.sigmoid(SWIGLU_ALPHA * gate_val) * route_weight[:, None]).astype(jnp.bfloat16)
            down_rows = lax.dynamic_slice_in_dim(down_weight, first_col, slice_width, 0)
            spread_mine = lax.dynamic_slice_in_dim(spread_moe, block_index * local_count * R, local_count * R, 1)
            up_rows = lax.dynamic_slice_in_dim(mixture_up, block_index * local_count, local_count, 0).reshape(local_count * R, D)
            term = jnp.dot(active, down_rows, preferred_element_type=jnp.float32) + jnp.dot(spread_mine, up_rows, preferred_element_type=jnp.float32)
            return (carry + settle(term), None)
        moe_sum, _ = lax.scan(moe_block, jnp.zeros((group_rows, D), jnp.float32), block_ids)
        return (hidden + moe_sum).astype(jnp.bfloat16)
    grouped = (tokens.reshape(N_ADAPTER, group_rows, D), lengths, prompt_adapter, expert_ids.reshape(N_ADAPTER, group_rows, TOP), expert_weights.reshape(N_ADAPTER, group_rows, TOP))
    return lax.map(one_group, grouped).reshape(N_ADAPTER * group_rows, D)
```

```python
import math

import jax
import jax.numpy as jnp
from jax import lax
from jax.sharding import Mesh, PartitionSpec as P

QH = 64
KVH = 8
HD = 64
FF = 2880
WINDOW = 128
TOP = 4
ROUTED = 32
R = 16
TENSOR = ("tz", "tx")


NORM_EPS = 1e-05
ROPE_BASE = 150000.0
SWIGLU_ALPHA = 1.702


def token_tables(length_row, adapter_row, first_row, row_count):
    prompt_ends = jnp.cumsum(length_row)
    prompt_starts = prompt_ends - length_row
    token_index = first_row + jnp.arange(row_count, dtype=jnp.int32)
    member = (token_index[:, None] >= prompt_starts[None, :]) & (
        token_index[:, None] < prompt_ends[None, :]
    )
    prompt_index = jnp.arange(length_row.shape[0], dtype=jnp.int32)
    segment = jnp.sum(jnp.where(member, prompt_index[None, :], 0), axis=1)
    prompt_begin = jnp.sum(jnp.where(member, prompt_starts[None, :], 0), axis=1)
    adapter = jnp.sum(jnp.where(member, adapter_row[None, :], 0), axis=1)
    return (segment, token_index - prompt_begin, adapter)


def settle(values):
    return lax.optimization_barrier(values.astype(jnp.bfloat16)).astype(jnp.float32)


def rms_scale(row_block, gain):
    wide = row_block.astype(jnp.float32)
    mean_square = jnp.mean(wide * wide, axis=-1, keepdims=True)
    return (wide * lax.rsqrt(mean_square + NORM_EPS) * gain).astype(jnp.bfloat16)


def rotate(head_rows, position):
    half_width = head_rows.shape[-1] // 2
    freqs = jnp.exp(-math.log(ROPE_BASE) * jnp.arange(half_width, dtype=jnp.float32) / half_width)
    angles = position.astype(jnp.float32)[:, None] * freqs[None, :]
    cosine = jnp.cos(angles)[:, None, :]
    sine_val = jnp.sin(angles)[:, None, :]
    first_half = head_rows[..., :half_width]
    second_half = head_rows[..., half_width:]
    return jnp.concatenate(
        [
            first_half * cosine - second_half * sine_val,
            second_half * cosine + first_half * sine_val,
        ],
        axis=-1,
    )


def spread_rank(onehot, rank_rows):
    return (onehot[:, :, None] * rank_rows[:, None, :]).reshape(rank_rows.shape[0], -1)


def attend(queries, key_rows, value_rows, segment, sink_logits):
    row_count = queries.shape[0]
    block_rows = min(512, row_count)
    key_pad = jnp.pad(key_rows, ((WINDOW, 0), (0, 0), (0, 0)))
    value_pad = jnp.pad(value_rows, ((WINDOW, 0), (0, 0), (0, 0)))
    segment_pad = jnp.pad(segment, (WINDOW, 0), constant_values=-1)
    sink_weight = jnp.exp(sink_logits)[:, None]
    score_scale = queries.shape[-1] ** (-0.5)

    def one_block(block_start):
        row_pos = jnp.arange(block_rows, dtype=jnp.int32)[:, None] + WINDOW
        col_pos = jnp.arange(block_rows + WINDOW, dtype=jnp.int32)[None, :]
        allowed = (
            (segment[:, None] == segment_pad[None, :])
            & (col_pos <= row_pos)
            & (row_pos - col_pos < WINDOW)
        )
        scores = (
            jnp.einsum("qhd,khd->hqk", queries, key_pad, preferred_element_type=jnp.float32)
            * score_scale
        )
        weights = jnp.where(allowed[None], jnp.exp(scores), 0.0)
        denominator = sink_weight + jnp.sum(weights, axis=-1)
        weights_bf = (weights / denominator[..., None]).astype(jnp.bfloat16)
        mixed_block = jnp.einsum(
            "hqk,khd->qhd", weights_bf, value_pad, preferred_element_type=jnp.float32
        )
        return mixed_block.astype(jnp.bfloat16).reshape(block_rows, -1)

    block_starts = jnp.arange(row_count // block_rows, dtype=jnp.int32) * block_rows
    return lax.map(one_block, block_starts).reshape(row_count, -1)


def tensor_index():
    return lax.axis_index("tz") * lax.axis_size("tx") + lax.axis_index("tx")


def tensor_size():
    return lax.axis_size("tz") * lax.axis_size("tx")


def gather_tensor(block, axis=0):
    inner = lax.all_gather(block, "tx", axis=axis, tiled=True)
    return lax.all_gather(inner, "tz", axis=axis, tiled=True)


def scatter_tensor(block):
    inner = lax.psum_scatter(block, "tz", scatter_dimension=0, tiled=True)
    return lax.psum_scatter(inner, "tx", scatter_dimension=0, tiled=True)


def swap_owner(outgoing):
    return lax.all_to_all(outgoing, "adapter", split_axis=0, concat_axis=0, tiled=True)


def gather_tokens(row_block):
    return gather_tensor(row_block)


def tensor_total(partial_value):
    return gather_tensor(scatter_tensor(partial_value.astype(jnp.bfloat16))).astype(jnp.float32)


def small_total(partial_value):
    inner = lax.psum(partial_value.astype(jnp.bfloat16), "tx")
    return lax.psum(inner, "tz").astype(jnp.float32)


def partial_sum(term_maker, own_rows):
    return scatter_tensor(
        term_maker(jnp.int32(0), tensor_size() * own_rows).astype(jnp.bfloat16)
    ).astype(jnp.float32)


def ask_owners(normed_own, bank, lengths, prompt_adapter, adapter_slot):
    own_rows = normed_own.shape[0]
    owner_count = lax.axis_size("adapter")
    owner_here = lax.axis_index("adapter")
    first_row = tensor_index() * own_rows
    stored, rank_width, width_d = bank.shape
    adapter_count = adapter_slot.shape[0]
    adapter_ids = jnp.arange(adapter_count, dtype=jnp.int32)

    def slots_of(length_row, adapter_row):
        adapter = token_tables(length_row, adapter_row, first_row, own_rows)[2]
        return jnp.sum(
            jnp.where(adapter[:, None] == adapter_ids[None, :], adapter_slot[None, :], 0), axis=1
        )

    all_slots = jax.vmap(slots_of)(lengths, prompt_adapter)
    own_slots = lax.dynamic_index_in_dim(all_slots, owner_here, 0, keepdims=False)
    route_mask = (own_slots // stored)[None, :] == jnp.arange(owner_count, dtype=jnp.int32)[:, None]
    outgoing = jnp.where(
        route_mask[:, :, None], normed_own[None, :, :], jnp.zeros((), jnp.bfloat16)
    )
    incoming = swap_owner(outgoing)
    local_slot = all_slots - owner_here * stored
    pick_hot = (
        local_slot[:, :, None] == jnp.arange(stored, dtype=jnp.int32)[None, None, :]
    ).astype(jnp.float32)
    flat_rows = incoming.reshape(owner_count * own_rows, width_d)
    projected = lax.dot_general(
        flat_rows,
        bank.reshape(stored * rank_width, width_d),
        (((1,), (1,)), ((), ())),
        preferred_element_type=jnp.float32,
    )
    projected = projected.reshape(owner_count, own_rows, stored, rank_width)
    answer = jnp.sum(projected * pick_hot[..., None], axis=2).astype(jnp.bfloat16)
    returned = swap_owner(answer.reshape(owner_count, own_rows * rank_width))
    return jnp.sum(
        returned.reshape(owner_count, own_rows, rank_width).astype(jnp.float32), axis=0
    ).astype(jnp.bfloat16)


def per_device(
    tokens,
    gain_attention,
    query_weight,
    keyval_weight,
    output_weight,
    sink_logits,
    heads_down,
    query_up,
    keyval_up,
    output_down,
    output_up,
    gain_mixture,
    gate_up_weight,
    down_weight,
    mixture_down,
    mixture_up,
    lengths,
    prompt_adapter,
    adapter_slot,
    expert_ids,
    expert_weights,
):
    own_rows = tokens.shape[0]
    tensor_here = tensor_index()
    group_here = lax.axis_index("adapter")
    group_rows = own_rows * tensor_size()
    adapter_count = adapter_slot.shape[0]
    query_cols = query_weight.shape[1]
    local_count = output_up.shape[0]
    slice_width = down_weight.shape[0]
    first_own = tensor_here * own_rows
    entries_here = keyval_weight.shape[2]
    length_row = lax.dynamic_index_in_dim(lengths, group_here, 0, keepdims=False)
    adapter_row = lax.dynamic_index_in_dim(prompt_adapter, group_here, 0, keepdims=False)
    segment, position, adapter = token_tables(length_row, adapter_row, jnp.int32(0), group_rows)
    adapter_hit = adapter[:, None] == jnp.arange(adapter_count, dtype=jnp.int32)[None, :]
    onehot = adapter_hit.astype(jnp.bfloat16)
    local_ids = tensor_here * local_count + jnp.arange(local_count, dtype=jnp.int32)
    local_hot = (adapter[:, None] == local_ids[None, :]).astype(jnp.bfloat16)
    normed_own = rms_scale(tokens, gain_attention)
    tokens_all = gather_tokens(tokens)
    normed = rms_scale(tokens_all, gain_attention)
    rank_own = ask_owners(normed_own, heads_down, lengths, prompt_adapter, adapter_slot)
    rank_qkv = gather_tokens(rank_own)
    queries = jnp.dot(normed, query_weight, preferred_element_type=jnp.float32)
    queries = queries + jnp.dot(
        spread_rank(onehot, rank_qkv[:, :R]),
        query_up.reshape(adapter_count * R, query_cols),
        preferred_element_type=jnp.float32,
    )
    queries = rotate(queries.reshape(group_rows, query_cols // HD, HD), position).astype(
        jnp.bfloat16
    )
    key_weight = keyval_weight[:, 0].reshape(keyval_weight.shape[0], entries_here * KVH)
    value_weight = keyval_weight[:, 1].reshape(keyval_weight.shape[0], entries_here * KVH)
    key_part = jnp.dot(normed, key_weight, preferred_element_type=jnp.float32)
    key_part = key_part + jnp.dot(
        spread_rank(onehot, rank_qkv[:, R : 2 * R]),
        keyval_up[:, 0].reshape(adapter_count * R, -1),
        preferred_element_type=jnp.float32,
    )
    value_part = jnp.dot(normed, value_weight, preferred_element_type=jnp.float32)
    value_part = value_part + jnp.dot(
        spread_rank(onehot, rank_qkv[:, 2 * R : 3 * R]),
        keyval_up[:, 1].reshape(adapter_count * R, -1),
        preferred_element_type=jnp.float32,
    )
    keyval_part = (
        jnp.stack([key_part, value_part], axis=1)
        .astype(jnp.bfloat16)
        .reshape(group_rows, 2, entries_here, KVH)
    )
    keyval_all = gather_tensor(keyval_part, axis=2)
    key_rows = rotate(
        jnp.transpose(keyval_all[:, 0].astype(jnp.float32), (0, 2, 1)), position
    ).astype(jnp.bfloat16)
    value_rows = jnp.transpose(keyval_all[:, 1], (0, 2, 1))
    heads_here = query_cols // HD
    head_map = (tensor_here * heads_here + jnp.arange(heads_here, dtype=jnp.int32)) // (QH // KVH)
    mixed_rows = attend(
        queries,
        jnp.take(key_rows, head_map, axis=1),
        jnp.take(value_rows, head_map, axis=1),
        segment,
        sink_logits,
    )
    rank_table = output_down.reshape(adapter_count * R, query_cols)
    rank_terms = lax.dot_general(
        mixed_rows, rank_table, (((1,), (1,)), ((), ())), preferred_element_type=jnp.float32
    )
    rank_terms = jnp.sum(
        rank_terms.reshape(group_rows, adapter_count, R) * onehot[:, :, None], axis=1
    )
    rank_out = small_total(settle(rank_terms)).astype(jnp.bfloat16)
    spread_out = spread_rank(local_hot, rank_out)
    up_out = output_up.reshape(local_count * R, -1)
    term = jnp.dot(mixed_rows, output_weight, preferred_element_type=jnp.float32)
    attn_all = tensor_total(
        settle(term + jnp.dot(spread_out, up_out, preferred_element_type=jnp.float32))
    )
    hidden_all = tokens_all.astype(jnp.float32) + attn_all
    normed_two = rms_scale(hidden_all, gain_mixture)
    hidden_own = lax.dynamic_slice_in_dim(hidden_all, first_own, own_rows, 0)
    normed_two_own = lax.dynamic_slice_in_dim(normed_two, first_own, own_rows, 0)
    rank_moe_own = ask_owners(normed_two_own, mixture_down, lengths, prompt_adapter, adapter_slot)
    rank_moe = gather_tokens(rank_moe_own)
    expert_here = tensor_here * slice_width // FF
    named = expert_ids == expert_here
    route_weight = jnp.sum(jnp.where(named, expert_weights, 0.0), axis=1)
    picked = jnp.any(named, axis=1)
    capacity = group_rows * TOP // ROUTED * 2
    order = jnp.cumsum(picked.astype(jnp.int32)) - 1
    target = jnp.where(picked, order, capacity)
    source = (
        jnp.zeros((capacity,), jnp.int32)
        .at[target]
        .set(jnp.arange(group_rows, dtype=jnp.int32), mode="drop")
    )
    slot_used = jnp.arange(capacity, dtype=jnp.int32) < jnp.sum(picked.astype(jnp.int32))
    compact_in = jnp.take(normed_two, source, axis=0)
    compact_route = jnp.where(slot_used, jnp.take(route_weight, source, axis=0), 0.0)
    gate_val = jnp.dot(compact_in, gate_up_weight[:, 0], preferred_element_type=jnp.float32)
    lift_val = jnp.dot(compact_in, gate_up_weight[:, 1], preferred_element_type=jnp.float32)
    active = (
        (lift_val + 1.0)
        * gate_val
        * jax.nn.sigmoid(SWIGLU_ALPHA * gate_val)
        * compact_route[:, None]
    ).astype(jnp.bfloat16)
    compact_terms = jnp.dot(active, down_weight, preferred_element_type=jnp.float32)
    spread_moe = spread_rank(local_hot, rank_moe)
    up_moe = mixture_up.reshape(local_count * R, -1)

    def moe_term(row_start, row_count):
        expert_rows = jnp.take(compact_terms, jnp.clip(order, 0, capacity - 1), axis=0)
        expert_rows = jnp.where(picked[:, None], expert_rows, 0.0)
        return settle(expert_rows + jnp.dot(spread_moe, up_moe, preferred_element_type=jnp.float32))

    moe_own = partial_sum(moe_term, own_rows)
    return (hidden_own + moe_own).astype(jnp.bfloat16)


def split_mesh(mesh):
    grid = mesh.devices
    tensor_count, adapter_count = grid.shape
    x_coords = {getattr(d, "coords", (i,))[0] for i, d in enumerate(grid[:, 0])}
    x_count = len(x_coords) if tensor_count % len(x_coords) == 0 else 1
    return Mesh(grid.reshape(tensor_count // x_count, x_count, adapter_count), ("tz", "tx", "adapter"))


def solution(mesh):
    mesh = split_mesh(mesh)
    in_specs = (
        P(("adapter", "tz", "tx"), None),
        P(),
        P(None, TENSOR),
        P(None, None, TENSOR, None),
        P(TENSOR, None),
        P(TENSOR),
        P("adapter", None, None),
        P(None, None, TENSOR),
        P(None, None, None, TENSOR, None),
        P(None, None, TENSOR),
        P(TENSOR, None, None),
        P(),
        P(None, None, TENSOR),
        P(TENSOR, None),
        P("adapter", None, None),
        P(TENSOR, None, None),
        P(),
        P(),
        P(),
        P("adapter", None),
        P("adapter", None),
    )
    out_specs = P(("adapter", "tz", "tx"), None)
    return jax.shard_map(
        per_device, mesh=mesh, in_specs=in_specs, out_specs=out_specs, check_vma=False
    )
```

```python
import math

import jax
import jax.numpy as jnp
from jax import lax
from jax.sharding import Mesh, PartitionSpec as P

QH = 64
KVH = 8
HD = 64
FF = 2880
WINDOW = 128
TOP = 4
ROUTED = 32
R = 16
TENSOR = ("tz", "tx")


NORM_EPS = 1e-05
ROPE_BASE = 150000.0
SWIGLU_ALPHA = 1.702


def token_tables(length_row, adapter_row, first_row, row_count):
    prompt_ends = jnp.cumsum(length_row)
    prompt_starts = prompt_ends - length_row
    token_index = first_row + jnp.arange(row_count, dtype=jnp.int32)
    member = (token_index[:, None] >= prompt_starts[None, :]) & (
        token_index[:, None] < prompt_ends[None, :]
    )
    prompt_index = jnp.arange(length_row.shape[0], dtype=jnp.int32)
    segment = jnp.sum(jnp.where(member, prompt_index[None, :], 0), axis=1)
    prompt_begin = jnp.sum(jnp.where(member, prompt_starts[None, :], 0), axis=1)
    adapter = jnp.sum(jnp.where(member, adapter_row[None, :], 0), axis=1)
    return (segment, token_index - prompt_begin, adapter)


def settle(values):
    return lax.optimization_barrier(values.astype(jnp.bfloat16)).astype(jnp.float32)


def rms_scale(row_block, gain):
    wide = row_block.astype(jnp.float32)
    mean_square = jnp.mean(wide * wide, axis=-1, keepdims=True)
    return (wide * lax.rsqrt(mean_square + NORM_EPS) * gain).astype(jnp.bfloat16)


def rotate(head_rows, position):
    half_width = head_rows.shape[-1] // 2
    freqs = jnp.exp(-math.log(ROPE_BASE) * jnp.arange(half_width, dtype=jnp.float32) / half_width)
    angles = position.astype(jnp.float32)[:, None] * freqs[None, :]
    cosine = jnp.cos(angles)[:, None, :]
    sine_val = jnp.sin(angles)[:, None, :]
    first_half = head_rows[..., :half_width]
    second_half = head_rows[..., half_width:]
    return jnp.concatenate(
        [
            first_half * cosine - second_half * sine_val,
            second_half * cosine + first_half * sine_val,
        ],
        axis=-1,
    )


def spread_rank(onehot, rank_rows):
    return (onehot[:, :, None] * rank_rows[:, None, :]).reshape(rank_rows.shape[0], -1)


def attend(queries, key_rows, value_rows, segment, sink_logits):
    row_count = queries.shape[0]
    block_rows = min(512, row_count)
    key_pad = jnp.pad(key_rows, ((WINDOW, 0), (0, 0), (0, 0)))
    value_pad = jnp.pad(value_rows, ((WINDOW, 0), (0, 0), (0, 0)))
    segment_pad = jnp.pad(segment, (WINDOW, 0), constant_values=-1)
    sink_weight = jnp.exp(sink_logits)[:, None]
    score_scale = queries.shape[-1] ** (-0.5)

    def one_block(block_start):
        row_pos = jnp.arange(block_rows, dtype=jnp.int32)[:, None] + WINDOW
        col_pos = jnp.arange(block_rows + WINDOW, dtype=jnp.int32)[None, :]
        allowed = (
            (segment[:, None] == segment_pad[None, :])
            & (col_pos <= row_pos)
            & (row_pos - col_pos < WINDOW)
        )
        scores = (
            jnp.einsum("qhd,khd->hqk", queries, key_pad, preferred_element_type=jnp.float32)
            * score_scale
        )
        weights = jnp.where(allowed[None], jnp.exp(scores), 0.0)
        denominator = sink_weight + jnp.sum(weights, axis=-1)
        weights_bf = (weights / denominator[..., None]).astype(jnp.bfloat16)
        mixed_block = jnp.einsum(
            "hqk,khd->qhd", weights_bf, value_pad, preferred_element_type=jnp.float32
        )
        return mixed_block.astype(jnp.bfloat16).reshape(block_rows, -1)

    block_starts = jnp.arange(row_count // block_rows, dtype=jnp.int32) * block_rows
    return lax.map(one_block, block_starts).reshape(row_count, -1)


def tensor_index():
    return lax.axis_index("tz") * lax.axis_size("tx") + lax.axis_index("tx")


def tensor_size():
    return lax.axis_size("tz") * lax.axis_size("tx")


def gather_tensor(block, axis=0):
    inner = lax.all_gather(block, "tx", axis=axis, tiled=True)
    return lax.all_gather(inner, "tz", axis=axis, tiled=True)


def scatter_tensor(block):
    inner = lax.psum_scatter(block, "tz", scatter_dimension=0, tiled=True)
    return lax.psum_scatter(inner, "tx", scatter_dimension=0, tiled=True)


def swap_owner(outgoing):
    return lax.all_to_all(outgoing, "adapter", split_axis=0, concat_axis=0, tiled=True)


def gather_tokens(row_block):
    return gather_tensor(row_block)


def tensor_total(partial_value):
    return gather_tensor(scatter_tensor(partial_value.astype(jnp.bfloat16))).astype(jnp.float32)


def small_total(partial_value):
    inner = lax.psum(partial_value.astype(jnp.bfloat16), "tx")
    return lax.psum(inner, "tz").astype(jnp.float32)


def partial_sum(term_maker, own_rows):
    return scatter_tensor(
        term_maker(jnp.int32(0), tensor_size() * own_rows).astype(jnp.bfloat16)
    ).astype(jnp.float32)


def ask_owners(normed_own, bank, lengths, prompt_adapter, adapter_slot):
    own_rows = normed_own.shape[0]
    owner_count = lax.axis_size("adapter")
    owner_here = lax.axis_index("adapter")
    first_row = tensor_index() * own_rows
    stored, rank_width, width_d = bank.shape
    adapter_count = adapter_slot.shape[0]
    adapter_ids = jnp.arange(adapter_count, dtype=jnp.int32)

    def slots_of(length_row, adapter_row):
        adapter = token_tables(length_row, adapter_row, first_row, own_rows)[2]
        return jnp.sum(
            jnp.where(adapter[:, None] == adapter_ids[None, :], adapter_slot[None, :], 0), axis=1
        )

    all_slots = jax.vmap(slots_of)(lengths, prompt_adapter)
    own_slots = lax.dynamic_index_in_dim(all_slots, owner_here, 0, keepdims=False)
    route_mask = (own_slots // stored)[None, :] == jnp.arange(owner_count, dtype=jnp.int32)[:, None]
    outgoing = jnp.where(
        route_mask[:, :, None], normed_own[None, :, :], jnp.zeros((), jnp.bfloat16)
    )
    incoming = swap_owner(outgoing)
    local_slot = all_slots - owner_here * stored
    pick_hot = (
        local_slot[:, :, None] == jnp.arange(stored, dtype=jnp.int32)[None, None, :]
    ).astype(jnp.float32)
    flat_rows = incoming.reshape(owner_count * own_rows, width_d)
    projected = lax.dot_general(
        flat_rows,
        bank.reshape(stored * rank_width, width_d),
        (((1,), (1,)), ((), ())),
        preferred_element_type=jnp.float32,
    )
    projected = projected.reshape(owner_count, own_rows, stored, rank_width)
    answer = jnp.sum(projected * pick_hot[..., None], axis=2).astype(jnp.bfloat16)
    returned = swap_owner(answer.reshape(owner_count, own_rows * rank_width))
    return jnp.sum(
        returned.reshape(owner_count, own_rows, rank_width).astype(jnp.float32), axis=0
    ).astype(jnp.bfloat16)


def per_device(
    tokens,
    gain_attention,
    query_weight,
    keyval_weight,
    output_weight,
    sink_logits,
    heads_down,
    query_up,
    keyval_up,
    output_down,
    output_up,
    gain_mixture,
    gate_up_weight,
    down_weight,
    mixture_down,
    mixture_up,
    lengths,
    prompt_adapter,
    adapter_slot,
    expert_ids,
    expert_weights,
):
    own_rows = tokens.shape[0]
    tensor_here = tensor_index()
    group_here = lax.axis_index("adapter")
    group_rows = own_rows * tensor_size()
    adapter_count = adapter_slot.shape[0]
    query_cols = query_weight.shape[1]
    local_count = output_up.shape[0]
    slice_width = down_weight.shape[0]
    first_own = tensor_here * own_rows
    entries_here = keyval_weight.shape[2]
    length_row = lax.dynamic_index_in_dim(lengths, group_here, 0, keepdims=False)
    adapter_row = lax.dynamic_index_in_dim(prompt_adapter, group_here, 0, keepdims=False)
    segment, position, adapter = token_tables(length_row, adapter_row, jnp.int32(0), group_rows)
    adapter_hit = adapter[:, None] == jnp.arange(adapter_count, dtype=jnp.int32)[None, :]
    onehot = adapter_hit.astype(jnp.bfloat16)
    local_ids = tensor_here * local_count + jnp.arange(local_count, dtype=jnp.int32)
    local_hot = (adapter[:, None] == local_ids[None, :]).astype(jnp.bfloat16)
    normed_own = rms_scale(tokens, gain_attention)
    tokens_all = gather_tokens(tokens)
    normed = rms_scale(tokens_all, gain_attention)
    rank_own = ask_owners(normed_own, heads_down, lengths, prompt_adapter, adapter_slot)
    rank_qkv = gather_tokens(rank_own)
    queries = jnp.dot(normed, query_weight, preferred_element_type=jnp.float32)
    queries = queries + jnp.dot(
        spread_rank(onehot, rank_qkv[:, :R]),
        query_up.reshape(adapter_count * R, query_cols),
        preferred_element_type=jnp.float32,
    )
    queries = rotate(queries.reshape(group_rows, query_cols // HD, HD), position).astype(
        jnp.bfloat16
    )
    heads_here = query_cols // HD
    tensor_count = tensor_size()
    dest_head = (jnp.arange(tensor_count, dtype=jnp.int32) * heads_here) // (QH // KVH)
    weight_send = jnp.moveaxis(jnp.take(keyval_weight, dest_head, axis=3), 3, 0)
    weight_recv = lax.all_to_all(weight_send, TENSOR, 0, 0, tiled=True)
    head_weight = jnp.transpose(weight_recv, (1, 2, 0, 3)).reshape(
        keyval_weight.shape[0], 2, tensor_count * entries_here
    )
    up_send = jnp.moveaxis(jnp.take(keyval_up, dest_head, axis=4), 4, 0)
    up_recv = lax.all_to_all(up_send, TENSOR, 0, 0, tiled=True)
    head_up = jnp.transpose(up_recv, (1, 2, 3, 0, 4)).reshape(
        adapter_count, 2, R, tensor_count * entries_here
    )
    key_part = jnp.dot(normed, head_weight[:, 0], preferred_element_type=jnp.float32)
    key_part = key_part + jnp.dot(
        spread_rank(onehot, rank_qkv[:, R : 2 * R]),
        head_up[:, 0].reshape(adapter_count * R, -1),
        preferred_element_type=jnp.float32,
    )
    value_part = jnp.dot(normed, head_weight[:, 1], preferred_element_type=jnp.float32)
    value_part = value_part + jnp.dot(
        spread_rank(onehot, rank_qkv[:, 2 * R : 3 * R]),
        head_up[:, 1].reshape(adapter_count * R, -1),
        preferred_element_type=jnp.float32,
    )
    key_rows = rotate(
        key_part.astype(jnp.bfloat16).astype(jnp.float32)[:, None, :], position
    ).astype(jnp.bfloat16)
    value_rows = value_part.astype(jnp.bfloat16)[:, None, :]
    mixed_rows = attend(
        queries,
        jnp.broadcast_to(key_rows, (group_rows, heads_here, HD)),
        jnp.broadcast_to(value_rows, (group_rows, heads_here, HD)),
        segment,
        sink_logits,
    )
    rank_table = output_down.reshape(adapter_count * R, query_cols)
    rank_terms = lax.dot_general(
        mixed_rows, rank_table, (((1,), (1,)), ((), ())), preferred_element_type=jnp.float32
    )
    rank_terms = jnp.sum(
        rank_terms.reshape(group_rows, adapter_count, R) * onehot[:, :, None], axis=1
    )
    rank_out = small_total(settle(rank_terms)).astype(jnp.bfloat16)
    spread_out = spread_rank(local_hot, rank_out)
    up_out = output_up.reshape(local_count * R, -1)
    term = jnp.dot(mixed_rows, output_weight, preferred_element_type=jnp.float32)
    attn_all = tensor_total(
        settle(term + jnp.dot(spread_out, up_out, preferred_element_type=jnp.float32))
    )
    hidden_all = tokens_all.astype(jnp.float32) + attn_all
    normed_two = rms_scale(hidden_all, gain_mixture)
    hidden_own = lax.dynamic_slice_in_dim(hidden_all, first_own, own_rows, 0)
    normed_two_own = lax.dynamic_slice_in_dim(normed_two, first_own, own_rows, 0)
    prompt_count = adapter_row.shape[0]
    owner_count = lax.axis_size("adapter")
    bank_send = jnp.broadcast_to(mixture_down[None], (owner_count,) + mixture_down.shape)
    bank_all = lax.all_to_all(bank_send, "adapter", 0, 0, tiled=True)
    bank_all = bank_all.reshape(-1, R, mixture_down.shape[-1])
    bank_group = jnp.take(bank_all, jnp.take(adapter_slot, adapter_row), axis=0)
    moe_proj = lax.dot_general(
        normed_two,
        bank_group.reshape(prompt_count * R, -1),
        (((1,), (1,)), ((), ())),
        preferred_element_type=jnp.float32,
    )
    segment_hot = (segment[:, None] == jnp.arange(prompt_count, dtype=jnp.int32)[None, :]).astype(
        jnp.float32
    )
    rank_moe = jnp.sum(
        moe_proj.reshape(group_rows, prompt_count, R) * segment_hot[:, :, None], axis=1
    ).astype(jnp.bfloat16)
    expert_here = tensor_here * slice_width // FF
    named = expert_ids == expert_here
    route_weight = jnp.sum(jnp.where(named, expert_weights, 0.0), axis=1)
    picked = jnp.any(named, axis=1)
    capacity = group_rows * TOP // ROUTED * 2
    order = jnp.cumsum(picked.astype(jnp.int32)) - 1
    target = jnp.where(picked, order, capacity)
    source = (
        jnp.zeros((capacity,), jnp.int32)
        .at[target]
        .set(jnp.arange(group_rows, dtype=jnp.int32), mode="drop")
    )
    slot_used = jnp.arange(capacity, dtype=jnp.int32) < jnp.sum(picked.astype(jnp.int32))
    compact_in = jnp.take(normed_two, source, axis=0)
    compact_route = jnp.where(slot_used, jnp.take(route_weight, source, axis=0), 0.0)
    gate_val = jnp.dot(compact_in, gate_up_weight[:, 0], preferred_element_type=jnp.float32)
    lift_val = jnp.dot(compact_in, gate_up_weight[:, 1], preferred_element_type=jnp.float32)
    active = (
        (lift_val + 1.0)
        * gate_val
        * jax.nn.sigmoid(SWIGLU_ALPHA * gate_val)
        * compact_route[:, None]
    ).astype(jnp.bfloat16)
    compact_terms = jnp.dot(active, down_weight, preferred_element_type=jnp.float32)
    spread_moe = spread_rank(local_hot, rank_moe)
    up_moe = mixture_up.reshape(local_count * R, -1)

    def moe_term(row_start, row_count):
        expert_rows = jnp.take(compact_terms, jnp.clip(order, 0, capacity - 1), axis=0)
        expert_rows = jnp.where(picked[:, None], expert_rows, 0.0)
        return settle(expert_rows + jnp.dot(spread_moe, up_moe, preferred_element_type=jnp.float32))

    moe_own = partial_sum(moe_term, own_rows)
    return (hidden_own + moe_own).astype(jnp.bfloat16)


def split_mesh(mesh):
    grid = mesh.devices
    tensor_count, adapter_count = grid.shape
    x_coords = {getattr(d, "coords", (i,))[0] for i, d in enumerate(grid[:, 0])}
    x_count = len(x_coords) if tensor_count % len(x_coords) == 0 else 1
    return Mesh(grid.reshape(tensor_count // x_count, x_count, adapter_count), ("tz", "tx", "adapter"))


def solution(mesh):
    mesh = split_mesh(mesh)
    in_specs = (
        P(("adapter", "tz", "tx"), None),
        P(),
        P(None, TENSOR),
        P(None, None, TENSOR, None),
        P(TENSOR, None),
        P(TENSOR),
        P("adapter", None, None),
        P(None, None, TENSOR),
        P(None, None, None, TENSOR, None),
        P(None, None, TENSOR),
        P(TENSOR, None, None),
        P(),
        P(None, None, TENSOR),
        P(TENSOR, None),
        P("adapter", None, None),
        P(TENSOR, None, None),
        P(),
        P(),
        P(),
        P("adapter", None),
        P("adapter", None),
    )
    out_specs = P(("adapter", "tz", "tx"), None)
    return jax.shard_map(
        per_device, mesh=mesh, in_specs=in_specs, out_specs=out_specs, check_vma=False
    )
```

```python
import math

import jax
import jax.numpy as jnp
from jax import lax
from jax.sharding import Mesh, PartitionSpec as P

QH = 64
KVH = 8
HD = 64
FF = 2880
WINDOW = 128
TOP = 4
ROUTED = 32
R = 16
TENSOR = ("tz", "tx")


NORM_EPS = 1e-05
ROPE_BASE = 150000.0
SWIGLU_ALPHA = 1.702


def token_tables(length_row, adapter_row, first_row, row_count):
    prompt_ends = jnp.cumsum(length_row)
    prompt_starts = prompt_ends - length_row
    token_index = first_row + jnp.arange(row_count, dtype=jnp.int32)
    member = (token_index[:, None] >= prompt_starts[None, :]) & (
        token_index[:, None] < prompt_ends[None, :]
    )
    prompt_index = jnp.arange(length_row.shape[0], dtype=jnp.int32)
    segment = jnp.sum(jnp.where(member, prompt_index[None, :], 0), axis=1)
    prompt_begin = jnp.sum(jnp.where(member, prompt_starts[None, :], 0), axis=1)
    adapter = jnp.sum(jnp.where(member, adapter_row[None, :], 0), axis=1)
    return (segment, token_index - prompt_begin, adapter)


def settle(values):
    return lax.optimization_barrier(values.astype(jnp.bfloat16)).astype(jnp.float32)


def rms_scale(row_block, gain):
    wide = row_block.astype(jnp.float32)
    mean_square = jnp.mean(wide * wide, axis=-1, keepdims=True)
    return (wide * lax.rsqrt(mean_square + NORM_EPS) * gain).astype(jnp.bfloat16)


def rotate(head_rows, position):
    half_width = head_rows.shape[-1] // 2
    freqs = jnp.exp(-math.log(ROPE_BASE) * jnp.arange(half_width, dtype=jnp.float32) / half_width)
    angles = position.astype(jnp.float32)[:, None] * freqs[None, :]
    cosine = jnp.cos(angles)[:, None, :]
    sine_val = jnp.sin(angles)[:, None, :]
    first_half = head_rows[..., :half_width]
    second_half = head_rows[..., half_width:]
    return jnp.concatenate(
        [
            first_half * cosine - second_half * sine_val,
            second_half * cosine + first_half * sine_val,
        ],
        axis=-1,
    )


def spread_rank(onehot, rank_rows):
    return (onehot[:, :, None] * rank_rows[:, None, :]).reshape(rank_rows.shape[0], -1)


def attend(queries, key_rows, value_rows, segment, sink_logits):
    row_count = queries.shape[0]
    block_rows = min(512, row_count)
    key_pad = jnp.pad(key_rows, ((WINDOW, 0), (0, 0), (0, 0)))
    value_pad = jnp.pad(value_rows, ((WINDOW, 0), (0, 0), (0, 0)))
    segment_pad = jnp.pad(segment, (WINDOW, 0), constant_values=-1)
    sink_weight = jnp.exp(sink_logits)[:, None]
    score_scale = queries.shape[-1] ** (-0.5)

    def one_block(block_start):
        row_pos = jnp.arange(block_rows, dtype=jnp.int32)[:, None] + WINDOW
        col_pos = jnp.arange(block_rows + WINDOW, dtype=jnp.int32)[None, :]
        allowed = (
            (segment[:, None] == segment_pad[None, :])
            & (col_pos <= row_pos)
            & (row_pos - col_pos < WINDOW)
        )
        scores = (
            jnp.einsum("qhd,khd->hqk", queries, key_pad, preferred_element_type=jnp.float32)
            * score_scale
        )
        weights = jnp.where(allowed[None], jnp.exp(scores), 0.0)
        denominator = sink_weight + jnp.sum(weights, axis=-1)
        weights_bf = (weights / denominator[..., None]).astype(jnp.bfloat16)
        mixed_block = jnp.einsum(
            "hqk,khd->qhd", weights_bf, value_pad, preferred_element_type=jnp.float32
        )
        return mixed_block.astype(jnp.bfloat16).reshape(block_rows, -1)

    block_starts = jnp.arange(row_count // block_rows, dtype=jnp.int32) * block_rows
    return lax.map(one_block, block_starts).reshape(row_count, -1)


def tensor_index():
    return lax.axis_index("tz") * lax.axis_size("tx") + lax.axis_index("tx")


def tensor_size():
    return lax.axis_size("tz") * lax.axis_size("tx")


def gather_tensor(block, axis=0):
    inner = lax.all_gather(block, "tx", axis=axis, tiled=True)
    return lax.all_gather(inner, "tz", axis=axis, tiled=True)


def scatter_tensor(block):
    inner = lax.psum_scatter(block, "tz", scatter_dimension=0, tiled=True)
    return lax.psum_scatter(inner, "tx", scatter_dimension=0, tiled=True)


def swap_owner(outgoing):
    return lax.all_to_all(outgoing, "adapter", split_axis=0, concat_axis=0, tiled=True)


def gather_tokens(row_block):
    return gather_tensor(row_block)


def tensor_total(partial_value):
    return gather_tensor(scatter_tensor(partial_value.astype(jnp.bfloat16))).astype(jnp.float32)


def small_total(partial_value):
    inner = lax.psum(partial_value.astype(jnp.bfloat16), "tx")
    return lax.psum(inner, "tz").astype(jnp.float32)


def partial_sum(term_maker, own_rows):
    return scatter_tensor(
        term_maker(jnp.int32(0), tensor_size() * own_rows).astype(jnp.bfloat16)
    ).astype(jnp.float32)


def ask_owners(normed_own, bank, lengths, prompt_adapter, adapter_slot):
    own_rows = normed_own.shape[0]
    owner_count = lax.axis_size("adapter")
    owner_here = lax.axis_index("adapter")
    first_row = tensor_index() * own_rows
    stored, rank_width, width_d = bank.shape
    adapter_count = adapter_slot.shape[0]
    adapter_ids = jnp.arange(adapter_count, dtype=jnp.int32)

    def slots_of(length_row, adapter_row):
        adapter = token_tables(length_row, adapter_row, first_row, own_rows)[2]
        return jnp.sum(
            jnp.where(adapter[:, None] == adapter_ids[None, :], adapter_slot[None, :], 0), axis=1
        )

    all_slots = jax.vmap(slots_of)(lengths, prompt_adapter)
    own_slots = lax.dynamic_index_in_dim(all_slots, owner_here, 0, keepdims=False)
    route_mask = (own_slots // stored)[None, :] == jnp.arange(owner_count, dtype=jnp.int32)[:, None]
    outgoing = jnp.where(
        route_mask[:, :, None], normed_own[None, :, :], jnp.zeros((), jnp.bfloat16)
    )
    incoming = swap_owner(outgoing)
    local_slot = all_slots - owner_here * stored
    pick_hot = (
        local_slot[:, :, None] == jnp.arange(stored, dtype=jnp.int32)[None, None, :]
    ).astype(jnp.float32)
    flat_rows = incoming.reshape(owner_count * own_rows, width_d)
    projected = lax.dot_general(
        flat_rows,
        bank.reshape(stored * rank_width, width_d),
        (((1,), (1,)), ((), ())),
        preferred_element_type=jnp.float32,
    )
    projected = projected.reshape(owner_count, own_rows, stored, rank_width)
    answer = jnp.sum(projected * pick_hot[..., None], axis=2).astype(jnp.bfloat16)
    returned = swap_owner(answer.reshape(owner_count, own_rows * rank_width))
    return jnp.sum(
        returned.reshape(owner_count, own_rows, rank_width).astype(jnp.float32), axis=0
    ).astype(jnp.bfloat16)


def per_device(
    tokens,
    gain_attention,
    query_weight,
    keyval_weight,
    output_weight,
    sink_logits,
    heads_down,
    query_up,
    keyval_up,
    output_down,
    output_up,
    gain_mixture,
    gate_up_weight,
    down_weight,
    mixture_down,
    mixture_up,
    lengths,
    prompt_adapter,
    adapter_slot,
    expert_ids,
    expert_weights,
):
    own_rows = tokens.shape[0]
    tensor_here = tensor_index()
    group_here = lax.axis_index("adapter")
    group_rows = own_rows * tensor_size()
    adapter_count = adapter_slot.shape[0]
    query_cols = query_weight.shape[1]
    local_count = output_up.shape[0]
    slice_width = down_weight.shape[0]
    first_own = tensor_here * own_rows
    entries_here = keyval_weight.shape[2]
    length_row = lax.dynamic_index_in_dim(lengths, group_here, 0, keepdims=False)
    adapter_row = lax.dynamic_index_in_dim(prompt_adapter, group_here, 0, keepdims=False)
    segment, position, adapter = token_tables(length_row, adapter_row, jnp.int32(0), group_rows)
    adapter_hit = adapter[:, None] == jnp.arange(adapter_count, dtype=jnp.int32)[None, :]
    onehot = adapter_hit.astype(jnp.bfloat16)
    local_ids = tensor_here * local_count + jnp.arange(local_count, dtype=jnp.int32)
    local_hot = (adapter[:, None] == local_ids[None, :]).astype(jnp.bfloat16)
    normed_own = rms_scale(tokens, gain_attention)
    tokens_all = gather_tokens(tokens)
    normed = rms_scale(tokens_all, gain_attention)
    rank_own = ask_owners(normed_own, heads_down, lengths, prompt_adapter, adapter_slot)
    rank_qkv = gather_tokens(rank_own)
    queries = jnp.dot(normed, query_weight, preferred_element_type=jnp.float32)
    queries = queries + jnp.dot(
        spread_rank(onehot, rank_qkv[:, :R]),
        query_up.reshape(adapter_count * R, query_cols),
        preferred_element_type=jnp.float32,
    )
    queries = rotate(queries.reshape(group_rows, query_cols // HD, HD), position).astype(
        jnp.bfloat16
    )
    heads_here = query_cols // HD
    tensor_count = tensor_size()
    dest_head = (jnp.arange(tensor_count, dtype=jnp.int32) * heads_here) // (QH // KVH)
    weight_send = jnp.moveaxis(jnp.take(keyval_weight, dest_head, axis=3), 3, 0)
    weight_recv = lax.all_to_all(weight_send, TENSOR, 0, 0, tiled=True)
    head_weight = jnp.transpose(weight_recv, (1, 2, 0, 3)).reshape(
        keyval_weight.shape[0], 2, tensor_count * entries_here
    )
    up_send = jnp.moveaxis(jnp.take(keyval_up, dest_head, axis=4), 4, 0)
    up_recv = lax.all_to_all(up_send, TENSOR, 0, 0, tiled=True)
    head_up = jnp.transpose(up_recv, (1, 2, 3, 0, 4)).reshape(
        adapter_count, 2, R, tensor_count * entries_here
    )
    key_part = jnp.dot(normed, head_weight[:, 0], preferred_element_type=jnp.float32)
    key_part = key_part + jnp.dot(
        spread_rank(onehot, rank_qkv[:, R : 2 * R]),
        head_up[:, 0].reshape(adapter_count * R, -1),
        preferred_element_type=jnp.float32,
    )
    value_part = jnp.dot(normed, head_weight[:, 1], preferred_element_type=jnp.float32)
    value_part = value_part + jnp.dot(
        spread_rank(onehot, rank_qkv[:, 2 * R : 3 * R]),
        head_up[:, 1].reshape(adapter_count * R, -1),
        preferred_element_type=jnp.float32,
    )
    key_rows = rotate(
        key_part.astype(jnp.bfloat16).astype(jnp.float32)[:, None, :], position
    ).astype(jnp.bfloat16)
    value_rows = value_part.astype(jnp.bfloat16)[:, None, :]
    mixed_rows = attend(
        queries,
        jnp.broadcast_to(key_rows, (group_rows, heads_here, HD)),
        jnp.broadcast_to(value_rows, (group_rows, heads_here, HD)),
        segment,
        sink_logits,
    )
    prompt_count = adapter_row.shape[0]
    owner_count = lax.axis_size("adapter")
    bank_send = jnp.broadcast_to(mixture_down[None], (owner_count,) + mixture_down.shape)
    bank_all = lax.all_to_all(bank_send, "adapter", 0, 0, tiled=True)
    bank_all = bank_all.reshape(-1, R, mixture_down.shape[-1])
    bank_all, mixed_rows = lax.optimization_barrier((bank_all, mixed_rows))
    rank_table = output_down.reshape(adapter_count * R, query_cols)
    rank_terms = lax.dot_general(
        mixed_rows, rank_table, (((1,), (1,)), ((), ())), preferred_element_type=jnp.float32
    )
    rank_terms = jnp.sum(
        rank_terms.reshape(group_rows, adapter_count, R) * onehot[:, :, None], axis=1
    )
    rank_out = small_total(settle(rank_terms)).astype(jnp.bfloat16)
    spread_out = spread_rank(local_hot, rank_out)
    up_out = output_up.reshape(local_count * R, -1)
    term = jnp.dot(mixed_rows, output_weight, preferred_element_type=jnp.float32)
    attn_all = tensor_total(
        settle(term + jnp.dot(spread_out, up_out, preferred_element_type=jnp.float32))
    )
    hidden_all = tokens_all.astype(jnp.float32) + attn_all
    normed_two = rms_scale(hidden_all, gain_mixture)
    hidden_own = lax.dynamic_slice_in_dim(hidden_all, first_own, own_rows, 0)
    normed_two_own = lax.dynamic_slice_in_dim(normed_two, first_own, own_rows, 0)
    bank_group = jnp.take(bank_all, jnp.take(adapter_slot, adapter_row), axis=0)
    moe_proj = lax.dot_general(
        normed_two,
        bank_group.reshape(prompt_count * R, -1),
        (((1,), (1,)), ((), ())),
        preferred_element_type=jnp.float32,
    )
    segment_hot = (segment[:, None] == jnp.arange(prompt_count, dtype=jnp.int32)[None, :]).astype(
        jnp.float32
    )
    rank_moe = jnp.sum(
        moe_proj.reshape(group_rows, prompt_count, R) * segment_hot[:, :, None], axis=1
    ).astype(jnp.bfloat16)
    expert_here = tensor_here * slice_width // FF
    named = expert_ids == expert_here
    route_weight = jnp.sum(jnp.where(named, expert_weights, 0.0), axis=1)
    picked = jnp.any(named, axis=1)
    gate_val = jnp.dot(normed_two, gate_up_weight[:, 0], preferred_element_type=jnp.float32)
    lift_val = jnp.dot(normed_two, gate_up_weight[:, 1], preferred_element_type=jnp.float32)
    active = (
        (lift_val + 1.0)
        * gate_val
        * jax.nn.sigmoid(SWIGLU_ALPHA * gate_val)
        * route_weight[:, None]
    ).astype(jnp.bfloat16)
    expert_terms = jnp.dot(active, down_weight, preferred_element_type=jnp.float32)
    spread_moe = spread_rank(local_hot, rank_moe)
    up_moe = mixture_up.reshape(local_count * R, -1)

    def moe_term(row_start, row_count):
        expert_rows = jnp.where(picked[:, None], expert_terms, 0.0)
        return settle(expert_rows + jnp.dot(spread_moe, up_moe, preferred_element_type=jnp.float32))

    moe_own = partial_sum(moe_term, own_rows)
    return (hidden_own + moe_own).astype(jnp.bfloat16)


def split_mesh(mesh):
    grid = mesh.devices
    tensor_count, adapter_count = grid.shape
    x_coords = {getattr(d, "coords", (i,))[0] for i, d in enumerate(grid[:, 0])}
    x_count = len(x_coords) if tensor_count % len(x_coords) == 0 else 1
    return Mesh(grid.reshape(tensor_count // x_count, x_count, adapter_count), ("tz", "tx", "adapter"))


def solution(mesh):
    mesh = split_mesh(mesh)
    in_specs = (
        P(("adapter", "tz", "tx"), None),
        P(),
        P(None, TENSOR),
        P(None, None, TENSOR, None),
        P(TENSOR, None),
        P(TENSOR),
        P("adapter", None, None),
        P(None, None, TENSOR),
        P(None, None, None, TENSOR, None),
        P(None, None, TENSOR),
        P(TENSOR, None, None),
        P(),
        P(None, None, TENSOR),
        P(TENSOR, None),
        P("adapter", None, None),
        P(TENSOR, None, None),
        P(),
        P(),
        P(),
        P("adapter", None),
        P("adapter", None),
    )
    out_specs = P(("adapter", "tz", "tx"), None)
    return jax.shard_map(
        per_device, mesh=mesh, in_specs=in_specs, out_specs=out_specs, check_vma=False
    )
```

```python
import math

import jax
import jax.numpy as jnp
from jax import lax
from jax.sharding import Mesh, PartitionSpec as P


QH = 64
KVH = 8
HD = 64
FF = 2880
WINDOW = 128
R = 16
TENSOR = ("tz", "tx")


NORM_EPS = 1e-05
ROPE_BASE = 150000.0
SWIGLU_ALPHA = 1.702


def token_tables(length_row, adapter_row, first_row, row_count):
    prompt_ends = jnp.cumsum(length_row)
    prompt_starts = prompt_ends - length_row
    token_index = first_row + jnp.arange(row_count, dtype=jnp.int32)
    member = (token_index[:, None] >= prompt_starts[None, :]) & (
        token_index[:, None] < prompt_ends[None, :]
    )
    prompt_index = jnp.arange(length_row.shape[0], dtype=jnp.int32)
    segment = jnp.sum(jnp.where(member, prompt_index[None, :], 0), axis=1)
    prompt_begin = jnp.sum(jnp.where(member, prompt_starts[None, :], 0), axis=1)
    adapter = jnp.sum(jnp.where(member, adapter_row[None, :], 0), axis=1)
    return (segment, token_index - prompt_begin, adapter)


def settle(values):
    return lax.optimization_barrier(values.astype(jnp.bfloat16)).astype(jnp.float32)


def rms_scale(row_block, gain):
    wide = row_block.astype(jnp.float32)
    mean_square = jnp.mean(wide * wide, axis=-1, keepdims=True)
    return (wide * lax.rsqrt(mean_square + NORM_EPS) * gain).astype(jnp.bfloat16)


def rotate(head_rows, position):
    half_width = head_rows.shape[-1] // 2
    freqs = jnp.exp(-math.log(ROPE_BASE) * jnp.arange(half_width, dtype=jnp.float32) / half_width)
    angles = position.astype(jnp.float32)[:, None] * freqs[None, :]
    cosine = jnp.cos(angles)[:, None, :]
    sine_val = jnp.sin(angles)[:, None, :]
    first_half = head_rows[..., :half_width]
    second_half = head_rows[..., half_width:]
    return jnp.concatenate(
        [
            first_half * cosine - second_half * sine_val,
            second_half * cosine + first_half * sine_val,
        ],
        axis=-1,
    )


def spread_rank(onehot, rank_rows):
    return (onehot[:, :, None] * rank_rows[:, None, :]).reshape(rank_rows.shape[0], -1)


def attend(queries, key_rows, value_rows, segment, sink_logits):
    row_count = queries.shape[0]
    block_rows = min(512, row_count)
    key_pad = jnp.pad(key_rows, ((WINDOW, 0), (0, 0), (0, 0)))
    value_pad = jnp.pad(value_rows, ((WINDOW, 0), (0, 0), (0, 0)))
    segment_pad = jnp.pad(segment, (WINDOW, 0), constant_values=-1)
    sink_weight = jnp.exp(sink_logits)[:, None]
    score_scale = queries.shape[-1] ** (-0.5)

    def one_block(block_start):
        row_pos = jnp.arange(block_rows, dtype=jnp.int32)[:, None] + WINDOW
        col_pos = jnp.arange(block_rows + WINDOW, dtype=jnp.int32)[None, :]
        allowed = (
            (segment[:, None] == segment_pad[None, :])
            & (col_pos <= row_pos)
            & (row_pos - col_pos < WINDOW)
        )
        scores = (
            jnp.einsum("qhd,khd->hqk", queries, key_pad, preferred_element_type=jnp.float32)
            * score_scale
        )
        weights = jnp.where(allowed[None], jnp.exp(scores), 0.0)
        denominator = sink_weight + jnp.sum(weights, axis=-1)
        weights_bf = (weights / denominator[..., None]).astype(jnp.bfloat16)
        mixed_block = jnp.einsum(
            "hqk,khd->qhd", weights_bf, value_pad, preferred_element_type=jnp.float32
        )
        return mixed_block.astype(jnp.bfloat16).reshape(block_rows, -1)

    block_starts = jnp.arange(row_count // block_rows, dtype=jnp.int32) * block_rows
    return lax.map(one_block, block_starts).reshape(row_count, -1)


def tensor_index():
    return lax.axis_index("tz") * lax.axis_size("tx") + lax.axis_index("tx")


def tensor_size():
    return lax.axis_size("tz") * lax.axis_size("tx")


def gather_tensor(block, axis=0):
    inner = lax.all_gather(block, "tx", axis=axis, tiled=True)
    return lax.all_gather(inner, "tz", axis=axis, tiled=True)


def scatter_tensor(block):
    inner = lax.psum_scatter(block, "tz", scatter_dimension=0, tiled=True)
    return lax.psum_scatter(inner, "tx", scatter_dimension=0, tiled=True)


def swap_owner(outgoing):
    return lax.all_to_all(outgoing, "adapter", split_axis=0, concat_axis=0, tiled=True)


def gather_tokens(row_block):
    return gather_tensor(row_block)


def tensor_total(partial_value):
    return gather_tensor(scatter_tensor(partial_value.astype(jnp.bfloat16))).astype(jnp.float32)


def partial_sum(term_maker, own_rows):
    return scatter_tensor(
        term_maker(jnp.int32(0), tensor_size() * own_rows).astype(jnp.bfloat16)
    ).astype(jnp.float32)


def ask_owners(normed_own, bank, lengths, prompt_adapter, adapter_slot):
    own_rows = normed_own.shape[0]
    owner_count = lax.axis_size("adapter")
    owner_here = lax.axis_index("adapter")
    first_row = tensor_index() * own_rows
    stored, rank_width, width_d = bank.shape
    adapter_count = adapter_slot.shape[0]
    adapter_ids = jnp.arange(adapter_count, dtype=jnp.int32)

    def slots_of(length_row, adapter_row):
        adapter = token_tables(length_row, adapter_row, first_row, own_rows)[2]
        return jnp.sum(
            jnp.where(adapter[:, None] == adapter_ids[None, :], adapter_slot[None, :], 0), axis=1
        )

    all_slots = jax.vmap(slots_of)(lengths, prompt_adapter)
    own_slots = lax.dynamic_index_in_dim(all_slots, owner_here, 0, keepdims=False)
    route_mask = (own_slots // stored)[None, :] == jnp.arange(owner_count, dtype=jnp.int32)[:, None]
    outgoing = jnp.where(
        route_mask[:, :, None], normed_own[None, :, :], jnp.zeros((), jnp.bfloat16)
    )
    incoming = swap_owner(outgoing)
    local_slot = all_slots - owner_here * stored
    pick_hot = (
        local_slot[:, :, None] == jnp.arange(stored, dtype=jnp.int32)[None, None, :]
    ).astype(jnp.float32)
    flat_rows = incoming.reshape(owner_count * own_rows, width_d)
    projected = lax.dot_general(
        flat_rows,
        bank.reshape(stored * rank_width, width_d),
        (((1,), (1,)), ((), ())),
        preferred_element_type=jnp.float32,
    )
    projected = projected.reshape(owner_count, own_rows, stored, rank_width)
    answer = jnp.sum(projected * pick_hot[..., None], axis=2).astype(jnp.bfloat16)
    returned = swap_owner(answer.reshape(owner_count, own_rows * rank_width))
    return jnp.sum(
        returned.reshape(owner_count, own_rows, rank_width).astype(jnp.float32), axis=0
    ).astype(jnp.bfloat16)


def layer(
    tokens,
    gain_attention,
    query_weight,
    keyval_weight,
    output_weight,
    sink_logits,
    heads_down,
    query_up,
    keyval_up,
    output_down,
    output_up,
    gain_mixture,
    gate_up_weight,
    down_weight,
    mixture_down,
    mixture_up,
    lengths,
    prompt_adapter,
    adapter_slot,
    expert_ids,
    expert_weights,
):
    own_rows = tokens.shape[0]
    tensor_here = tensor_index()
    group_here = lax.axis_index("adapter")
    group_rows = own_rows * tensor_size()
    adapter_count = adapter_slot.shape[0]
    query_cols = query_weight.shape[1]
    local_count = output_up.shape[0]
    slice_width = down_weight.shape[0]
    first_own = tensor_here * own_rows
    entries_here = keyval_weight.shape[2]
    length_row = lax.dynamic_index_in_dim(lengths, group_here, 0, keepdims=False)
    adapter_row = lax.dynamic_index_in_dim(prompt_adapter, group_here, 0, keepdims=False)
    segment, position, adapter = token_tables(length_row, adapter_row, jnp.int32(0), group_rows)
    adapter_hit = adapter[:, None] == jnp.arange(adapter_count, dtype=jnp.int32)[None, :]
    onehot = adapter_hit.astype(jnp.bfloat16)
    local_ids = tensor_here * local_count + jnp.arange(local_count, dtype=jnp.int32)
    local_hot = (adapter[:, None] == local_ids[None, :]).astype(jnp.bfloat16)
    normed_own = rms_scale(tokens, gain_attention)
    tokens_all = gather_tokens(tokens)
    prompt_count = adapter_row.shape[0]
    owned = (adapter_row // local_count) == tensor_here
    up_pick = jnp.take(output_up, adapter_row % local_count, axis=0)
    up_pick = jnp.where(owned[:, None, None], up_pick, jnp.zeros((), up_pick.dtype))
    up_group = tensor_total(up_pick.reshape(prompt_count * R, -1)).astype(jnp.bfloat16)
    normed = rms_scale(tokens_all, gain_attention)
    rank_own = ask_owners(normed_own, heads_down, lengths, prompt_adapter, adapter_slot)
    rank_qkv = gather_tokens(rank_own)
    queries = jnp.dot(normed, query_weight, preferred_element_type=jnp.float32)
    queries = queries + jnp.dot(
        spread_rank(onehot, rank_qkv[:, :R]),
        query_up.reshape(adapter_count * R, query_cols),
        preferred_element_type=jnp.float32,
    )
    queries = rotate(queries.reshape(group_rows, query_cols // HD, HD), position).astype(
        jnp.bfloat16
    )
    heads_here = query_cols // HD
    tensor_count = tensor_size()
    dest_head = (jnp.arange(tensor_count, dtype=jnp.int32) * heads_here) // (QH // KVH)
    weight_send = jnp.moveaxis(jnp.take(keyval_weight, dest_head, axis=3), 3, 0)
    weight_recv = lax.all_to_all(weight_send, TENSOR, 0, 0, tiled=True)
    head_weight = jnp.transpose(weight_recv, (1, 2, 0, 3)).reshape(
        keyval_weight.shape[0], 2, tensor_count * entries_here
    )
    up_send = jnp.moveaxis(jnp.take(keyval_up, dest_head, axis=4), 4, 0)
    up_recv = lax.all_to_all(up_send, TENSOR, 0, 0, tiled=True)
    head_up = jnp.transpose(up_recv, (1, 2, 3, 0, 4)).reshape(
        adapter_count, 2, R, tensor_count * entries_here
    )
    key_part = jnp.dot(normed, head_weight[:, 0], preferred_element_type=jnp.float32)
    key_part = key_part + jnp.dot(
        spread_rank(onehot, rank_qkv[:, R : 2 * R]),
        head_up[:, 0].reshape(adapter_count * R, -1),
        preferred_element_type=jnp.float32,
    )
    value_part = jnp.dot(normed, head_weight[:, 1], preferred_element_type=jnp.float32)
    value_part = value_part + jnp.dot(
        spread_rank(onehot, rank_qkv[:, 2 * R : 3 * R]),
        head_up[:, 1].reshape(adapter_count * R, -1),
        preferred_element_type=jnp.float32,
    )
    key_rows = rotate(
        key_part.astype(jnp.bfloat16).astype(jnp.float32)[:, None, :], position
    ).astype(jnp.bfloat16)
    value_rows = value_part.astype(jnp.bfloat16)[:, None, :]
    mixed_rows = attend(
        queries,
        jnp.broadcast_to(key_rows, (group_rows, heads_here, HD)),
        jnp.broadcast_to(value_rows, (group_rows, heads_here, HD)),
        segment,
        sink_logits,
    )
    owner_count = lax.axis_size("adapter")
    bank_send = jnp.broadcast_to(mixture_down[None], (owner_count,) + mixture_down.shape)
    bank_all = lax.all_to_all(bank_send, "adapter", 0, 0, tiled=True)
    bank_all = bank_all.reshape(-1, R, mixture_down.shape[-1])
    rank_table = output_down.reshape(adapter_count * R, query_cols)
    rank_terms = lax.dot_general(
        mixed_rows, rank_table, (((1,), (1,)), ((), ())), preferred_element_type=jnp.float32
    )
    rank_terms = jnp.sum(
        rank_terms.reshape(group_rows, adapter_count, R) * onehot[:, :, None], axis=1
    )
    prompt_hot = (segment[:, None] == jnp.arange(prompt_count, dtype=jnp.int32)[None, :]).astype(
        jnp.bfloat16
    )
    spread_out = spread_rank(prompt_hot, settle(rank_terms).astype(jnp.bfloat16))
    term = jnp.dot(mixed_rows, output_weight, preferred_element_type=jnp.float32)
    attn_all = tensor_total(
        settle(
            term
            + jnp.dot(
                spread_out,
                up_group.reshape(prompt_count * R, -1),
                preferred_element_type=jnp.float32,
            )
        )
    )
    hidden_all = tokens_all.astype(jnp.float32) + attn_all
    normed_two = rms_scale(hidden_all, gain_mixture)
    hidden_own = lax.dynamic_slice_in_dim(hidden_all, first_own, own_rows, 0)
    normed_two_own = lax.dynamic_slice_in_dim(normed_two, first_own, own_rows, 0)
    bank_group = jnp.take(bank_all, jnp.take(adapter_slot, adapter_row), axis=0)
    moe_proj = lax.dot_general(
        normed_two,
        bank_group.reshape(prompt_count * R, -1),
        (((1,), (1,)), ((), ())),
        preferred_element_type=jnp.float32,
    )
    segment_hot = (segment[:, None] == jnp.arange(prompt_count, dtype=jnp.int32)[None, :]).astype(
        jnp.float32
    )
    rank_moe = jnp.sum(
        moe_proj.reshape(group_rows, prompt_count, R) * segment_hot[:, :, None], axis=1
    ).astype(jnp.bfloat16)
    expert_here = tensor_here * slice_width // FF
    named = expert_ids == expert_here
    route_weight = jnp.sum(jnp.where(named, expert_weights, 0.0), axis=1)
    picked = jnp.any(named, axis=1)
    gate_val = jnp.dot(normed_two, gate_up_weight[:, 0], preferred_element_type=jnp.float32)
    lift_val = jnp.dot(normed_two, gate_up_weight[:, 1], preferred_element_type=jnp.float32)
    active = (
        (lift_val + 1.0)
        * gate_val
        * jax.nn.sigmoid(SWIGLU_ALPHA * gate_val)
        * route_weight[:, None]
    ).astype(jnp.bfloat16)
    expert_terms = jnp.dot(active, down_weight, preferred_element_type=jnp.float32)
    spread_moe = spread_rank(local_hot, rank_moe)
    up_moe = mixture_up.reshape(local_count * R, -1)

    def moe_term(row_start, row_count):
        expert_rows = jnp.where(picked[:, None], expert_terms, 0.0)
        return settle(expert_rows + jnp.dot(spread_moe, up_moe, preferred_element_type=jnp.float32))

    moe_own = partial_sum(moe_term, own_rows)
    return (hidden_own + moe_own).astype(jnp.bfloat16)


def split_mesh(mesh):
    grid = mesh.devices
    tensor_count, adapter_count = grid.shape
    x_coords = {getattr(d, "coords", (i,))[0] for i, d in enumerate(grid[:, 0])}
    x_count = len(x_coords) if tensor_count % len(x_coords) == 0 else 1
    return Mesh(grid.reshape(tensor_count // x_count, x_count, adapter_count), ("tz", "tx", "adapter"))


def solution(mesh):
    mesh = split_mesh(mesh)
    in_specs = (
        P(("adapter", "tz", "tx"), None),
        P(),
        P(None, TENSOR),
        P(None, None, TENSOR, None),
        P(TENSOR, None),
        P(TENSOR),
        P("adapter", None, None),
        P(None, None, TENSOR),
        P(None, None, None, TENSOR, None),
        P(None, None, TENSOR),
        P(TENSOR, None, None),
        P(),
        P(None, None, TENSOR),
        P(TENSOR, None),
        P("adapter", None, None),
        P(TENSOR, None, None),
        P(),
        P(),
        P(),
        P("adapter", None),
        P("adapter", None),
    )
    out_specs = P(("adapter", "tz", "tx"), None)
    return jax.shard_map(layer, mesh=mesh, in_specs=in_specs, out_specs=out_specs, check_vma=False)
```

```python
import math

import jax
import jax.numpy as jnp
from jax import lax
from jax.sharding import Mesh, PartitionSpec as P

QH = 64
KVH = 8
HD = 64
FF = 2880
WINDOW = 128
R = 16
TENSOR = ("tz", "tx")


NORM_EPS = 1e-05
ROPE_BASE = 150000.0
SWIGLU_ALPHA = 1.702


def token_tables(length_row, adapter_row, first_row, row_count):
    prompt_ends = jnp.cumsum(length_row)
    prompt_starts = prompt_ends - length_row
    token_index = first_row + jnp.arange(row_count, dtype=jnp.int32)
    member = (token_index[:, None] >= prompt_starts[None, :]) & (
        token_index[:, None] < prompt_ends[None, :]
    )
    prompt_index = jnp.arange(length_row.shape[0], dtype=jnp.int32)
    segment = jnp.sum(jnp.where(member, prompt_index[None, :], 0), axis=1)
    prompt_begin = jnp.sum(jnp.where(member, prompt_starts[None, :], 0), axis=1)
    adapter = jnp.sum(jnp.where(member, adapter_row[None, :], 0), axis=1)
    return (segment, token_index - prompt_begin, adapter)


def settle(values):
    return lax.optimization_barrier(values.astype(jnp.bfloat16)).astype(jnp.float32)


def rms_scale(row_block, gain):
    wide = row_block.astype(jnp.float32)
    mean_square = jnp.mean(wide * wide, axis=-1, keepdims=True)
    return (wide * lax.rsqrt(mean_square + NORM_EPS) * gain).astype(jnp.bfloat16)


def rotate(head_rows, position):
    half_width = head_rows.shape[-1] // 2
    freqs = jnp.exp(-math.log(ROPE_BASE) * jnp.arange(half_width, dtype=jnp.float32) / half_width)
    angles = position.astype(jnp.float32)[:, None] * freqs[None, :]
    cosine = jnp.cos(angles)[:, None, :]
    sine_val = jnp.sin(angles)[:, None, :]
    first_half = head_rows[..., :half_width]
    second_half = head_rows[..., half_width:]
    return jnp.concatenate(
        [
            first_half * cosine - second_half * sine_val,
            second_half * cosine + first_half * sine_val,
        ],
        axis=-1,
    )


def spread_rank(onehot, rank_rows):
    return (onehot[:, :, None] * rank_rows[:, None, :]).reshape(rank_rows.shape[0], -1)


def attend(queries, key_rows, value_rows, segment, sink_logits):
    row_count = queries.shape[0]
    block_rows = min(512, row_count)
    key_pad = jnp.pad(key_rows, ((WINDOW, 0), (0, 0), (0, 0)))
    value_pad = jnp.pad(value_rows, ((WINDOW, 0), (0, 0), (0, 0)))
    segment_pad = jnp.pad(segment, (WINDOW, 0), constant_values=-1)
    sink_weight = jnp.exp(sink_logits)[:, None]
    score_scale = queries.shape[-1] ** (-0.5)

    def one_block(block_start):
        row_pos = jnp.arange(block_rows, dtype=jnp.int32)[:, None] + WINDOW
        col_pos = jnp.arange(block_rows + WINDOW, dtype=jnp.int32)[None, :]
        allowed = (
            (segment[:, None] == segment_pad[None, :])
            & (col_pos <= row_pos)
            & (row_pos - col_pos < WINDOW)
        )
        scores = (
            jnp.einsum("qhd,khd->hqk", queries, key_pad, preferred_element_type=jnp.float32)
            * score_scale
        )
        weights = jnp.where(allowed[None], jnp.exp(scores), 0.0)
        denominator = sink_weight + jnp.sum(weights, axis=-1)
        weights_bf = (weights / denominator[..., None]).astype(jnp.bfloat16)
        mixed_block = jnp.einsum(
            "hqk,khd->qhd", weights_bf, value_pad, preferred_element_type=jnp.float32
        )
        return mixed_block.astype(jnp.bfloat16).reshape(block_rows, -1)

    block_starts = jnp.arange(row_count // block_rows, dtype=jnp.int32) * block_rows
    return lax.map(one_block, block_starts).reshape(row_count, -1)


def tensor_index():
    return lax.axis_index("tz") * lax.axis_size("tx") + lax.axis_index("tx")


def tensor_size():
    return lax.axis_size("tz") * lax.axis_size("tx")


def gather_tensor(block, axis=0):
    inner = lax.all_gather(block, "tx", axis=axis, tiled=True)
    return lax.all_gather(inner, "tz", axis=axis, tiled=True)


def scatter_tensor(block):
    inner = lax.psum_scatter(block, "tz", scatter_dimension=0, tiled=True)
    return lax.psum_scatter(inner, "tx", scatter_dimension=0, tiled=True)


def swap_owner(outgoing):
    return lax.all_to_all(outgoing, "adapter", split_axis=0, concat_axis=0, tiled=True)


def gather_tokens(row_block):
    return gather_tensor(row_block)


def tensor_total(partial_value):
    return gather_tensor(scatter_tensor(partial_value.astype(jnp.bfloat16))).astype(jnp.float32)


def small_total(partial_value):
    inner = lax.psum(partial_value.astype(jnp.bfloat16), "tx")
    return lax.psum(inner, "tz").astype(jnp.float32)


def partial_sum(term_maker, own_rows):
    return scatter_tensor(
        term_maker(jnp.int32(0), tensor_size() * own_rows).astype(jnp.bfloat16)
    ).astype(jnp.float32)


def ask_owners(normed_own, bank, lengths, prompt_adapter, adapter_slot):
    own_rows = normed_own.shape[0]
    owner_count = lax.axis_size("adapter")
    owner_here = lax.axis_index("adapter")
    first_row = tensor_index() * own_rows
    stored, rank_width, width_d = bank.shape
    adapter_count = adapter_slot.shape[0]
    adapter_ids = jnp.arange(adapter_count, dtype=jnp.int32)

    def slots_of(length_row, adapter_row):
        adapter = token_tables(length_row, adapter_row, first_row, own_rows)[2]
        return jnp.sum(
            jnp.where(adapter[:, None] == adapter_ids[None, :], adapter_slot[None, :], 0), axis=1
        )

    all_slots = jax.vmap(slots_of)(lengths, prompt_adapter)
    own_slots = lax.dynamic_index_in_dim(all_slots, owner_here, 0, keepdims=False)
    route_mask = (own_slots // stored)[None, :] == jnp.arange(owner_count, dtype=jnp.int32)[:, None]
    outgoing = jnp.where(
        route_mask[:, :, None], normed_own[None, :, :], jnp.zeros((), jnp.bfloat16)
    )
    incoming = swap_owner(outgoing)
    local_slot = all_slots - owner_here * stored
    pick_hot = (
        local_slot[:, :, None] == jnp.arange(stored, dtype=jnp.int32)[None, None, :]
    ).astype(jnp.float32)
    flat_rows = incoming.reshape(owner_count * own_rows, width_d)
    projected = lax.dot_general(
        flat_rows,
        bank.reshape(stored * rank_width, width_d),
        (((1,), (1,)), ((), ())),
        preferred_element_type=jnp.float32,
    )
    projected = projected.reshape(owner_count, own_rows, stored, rank_width)
    answer = jnp.sum(projected * pick_hot[..., None], axis=2).astype(jnp.bfloat16)
    returned = swap_owner(answer.reshape(owner_count, own_rows * rank_width))
    return jnp.sum(
        returned.reshape(owner_count, own_rows, rank_width).astype(jnp.float32), axis=0
    ).astype(jnp.bfloat16)


def layer(
    tokens,
    gain_attention,
    query_weight,
    keyval_weight,
    output_weight,
    sink_logits,
    heads_down,
    query_up,
    keyval_up,
    output_down,
    output_up,
    gain_mixture,
    gate_up_weight,
    down_weight,
    mixture_down,
    mixture_up,
    lengths,
    prompt_adapter,
    adapter_slot,
    expert_ids,
    expert_weights,
):
    own_rows = tokens.shape[0]
    tensor_here = tensor_index()
    group_here = lax.axis_index("adapter")
    group_rows = own_rows * tensor_size()
    adapter_count = adapter_slot.shape[0]
    query_cols = query_weight.shape[1]
    local_count = output_up.shape[0]
    slice_width = down_weight.shape[0]
    first_own = tensor_here * own_rows
    entries_here = keyval_weight.shape[2]
    length_row = lax.dynamic_index_in_dim(lengths, group_here, 0, keepdims=False)
    adapter_row = lax.dynamic_index_in_dim(prompt_adapter, group_here, 0, keepdims=False)
    segment, position, adapter = token_tables(length_row, adapter_row, jnp.int32(0), group_rows)
    adapter_hit = adapter[:, None] == jnp.arange(adapter_count, dtype=jnp.int32)[None, :]
    onehot = adapter_hit.astype(jnp.bfloat16)
    local_ids = tensor_here * local_count + jnp.arange(local_count, dtype=jnp.int32)
    local_hot = (adapter[:, None] == local_ids[None, :]).astype(jnp.bfloat16)
    normed_own = rms_scale(tokens, gain_attention)
    tokens_all = gather_tokens(tokens)
    normed = rms_scale(tokens_all, gain_attention)
    rank_own = ask_owners(normed_own, heads_down, lengths, prompt_adapter, adapter_slot)
    rank_qkv = gather_tokens(rank_own)
    queries = jnp.dot(normed, query_weight, preferred_element_type=jnp.float32)
    queries = queries + jnp.dot(
        spread_rank(onehot, rank_qkv[:, :R]),
        query_up.reshape(adapter_count * R, query_cols),
        preferred_element_type=jnp.float32,
    )
    queries = rotate(queries.reshape(group_rows, query_cols // HD, HD), position).astype(
        jnp.bfloat16
    )
    heads_here = query_cols // HD
    tensor_count = tensor_size()
    dest_head = (jnp.arange(tensor_count, dtype=jnp.int32) * heads_here) // (QH // KVH)
    weight_send = jnp.moveaxis(jnp.take(keyval_weight, dest_head, axis=3), 3, 0)
    weight_recv = lax.all_to_all(weight_send, TENSOR, 0, 0, tiled=True)
    head_weight = jnp.transpose(weight_recv, (1, 2, 0, 3)).reshape(
        keyval_weight.shape[0], 2, tensor_count * entries_here
    )
    up_send = jnp.moveaxis(jnp.take(keyval_up, dest_head, axis=4), 4, 0)
    up_recv = lax.all_to_all(up_send, TENSOR, 0, 0, tiled=True)
    head_up = jnp.transpose(up_recv, (1, 2, 3, 0, 4)).reshape(
        adapter_count, 2, R, tensor_count * entries_here
    )
    key_part = jnp.dot(normed, head_weight[:, 0], preferred_element_type=jnp.float32)
    key_part = key_part + jnp.dot(
        spread_rank(onehot, rank_qkv[:, R : 2 * R]),
        head_up[:, 0].reshape(adapter_count * R, -1),
        preferred_element_type=jnp.float32,
    )
    value_part = jnp.dot(normed, head_weight[:, 1], preferred_element_type=jnp.float32)
    value_part = value_part + jnp.dot(
        spread_rank(onehot, rank_qkv[:, 2 * R : 3 * R]),
        head_up[:, 1].reshape(adapter_count * R, -1),
        preferred_element_type=jnp.float32,
    )
    key_rows = rotate(
        key_part.astype(jnp.bfloat16).astype(jnp.float32)[:, None, :], position
    ).astype(jnp.bfloat16)
    value_rows = value_part.astype(jnp.bfloat16)[:, None, :]
    mixed_rows = attend(
        queries,
        jnp.broadcast_to(key_rows, (group_rows, heads_here, HD)),
        jnp.broadcast_to(value_rows, (group_rows, heads_here, HD)),
        segment,
        sink_logits,
    )
    prompt_count = adapter_row.shape[0]
    owner_count = lax.axis_size("adapter")
    bank_send = jnp.broadcast_to(mixture_down[None], (owner_count,) + mixture_down.shape)
    bank_all = lax.all_to_all(bank_send, "adapter", 0, 0, tiled=True)
    bank_all = bank_all.reshape(-1, R, mixture_down.shape[-1])
    rank_table = output_down.reshape(adapter_count * R, query_cols)
    rank_terms = lax.dot_general(
        mixed_rows, rank_table, (((1,), (1,)), ((), ())), preferred_element_type=jnp.float32
    )
    rank_terms = jnp.sum(
        rank_terms.reshape(group_rows, adapter_count, R) * onehot[:, :, None], axis=1
    )
    rank_out = small_total(settle(rank_terms)).astype(jnp.bfloat16)
    spread_out = spread_rank(local_hot, rank_out)
    up_out = output_up.reshape(local_count * R, -1)
    term = jnp.dot(mixed_rows, output_weight, preferred_element_type=jnp.float32)
    attn_all = tensor_total(
        settle(term + jnp.dot(spread_out, up_out, preferred_element_type=jnp.float32))
    )
    hidden_all = tokens_all.astype(jnp.float32) + attn_all
    normed_two = rms_scale(hidden_all, gain_mixture)
    hidden_own = lax.dynamic_slice_in_dim(hidden_all, first_own, own_rows, 0)
    normed_two_own = lax.dynamic_slice_in_dim(normed_two, first_own, own_rows, 0)
    bank_group = jnp.take(bank_all, jnp.take(adapter_slot, adapter_row), axis=0)
    moe_proj = lax.dot_general(
        normed_two,
        bank_group.reshape(prompt_count * R, -1),
        (((1,), (1,)), ((), ())),
        preferred_element_type=jnp.float32,
    )
    segment_hot = (segment[:, None] == jnp.arange(prompt_count, dtype=jnp.int32)[None, :]).astype(
        jnp.float32
    )
    rank_moe = jnp.sum(
        moe_proj.reshape(group_rows, prompt_count, R) * segment_hot[:, :, None], axis=1
    ).astype(jnp.bfloat16)
    expert_here = tensor_here * slice_width // FF
    named = expert_ids == expert_here
    route_weight = jnp.sum(jnp.where(named, expert_weights, 0.0), axis=1)
    picked = jnp.any(named, axis=1)
    gate_val = jnp.dot(normed_two, gate_up_weight[:, 0], preferred_element_type=jnp.float32)
    lift_val = jnp.dot(normed_two, gate_up_weight[:, 1], preferred_element_type=jnp.float32)
    active = (
        (lift_val + 1.0)
        * gate_val
        * jax.nn.sigmoid(SWIGLU_ALPHA * gate_val)
        * route_weight[:, None]
    ).astype(jnp.bfloat16)
    expert_terms = jnp.dot(active, down_weight, preferred_element_type=jnp.float32)
    spread_moe = spread_rank(local_hot, rank_moe)
    up_moe = mixture_up.reshape(local_count * R, -1)

    def moe_term(row_start, row_count):
        expert_rows = jnp.where(picked[:, None], expert_terms, 0.0)
        return settle(expert_rows + jnp.dot(spread_moe, up_moe, preferred_element_type=jnp.float32))

    moe_own = partial_sum(moe_term, own_rows)
    return (hidden_own + moe_own).astype(jnp.bfloat16)


def split_mesh(mesh):
    grid = mesh.devices
    tensor_count, adapter_count = grid.shape
    x_coords = {getattr(d, "coords", (i,))[0] for i, d in enumerate(grid[:, 0])}
    x_count = len(x_coords) if tensor_count % len(x_coords) == 0 else 1
    return Mesh(grid.reshape(tensor_count // x_count, x_count, adapter_count), ("tz", "tx", "adapter"))


def solution(mesh):
    mesh = split_mesh(mesh)
    in_specs = (
        P(("adapter", "tz", "tx"), None),
        P(),
        P(None, TENSOR),
        P(None, None, TENSOR, None),
        P(TENSOR, None),
        P(TENSOR),
        P("adapter", None, None),
        P(None, None, TENSOR),
        P(None, None, None, TENSOR, None),
        P(None, None, TENSOR),
        P(TENSOR, None, None),
        P(),
        P(None, None, TENSOR),
        P(TENSOR, None),
        P("adapter", None, None),
        P(TENSOR, None, None),
        P(),
        P(),
        P(),
        P("adapter", None),
        P("adapter", None),
    )
    out_specs = P(("adapter", "tz", "tx"), None)
    return jax.shard_map(layer, mesh=mesh, in_specs=in_specs, out_specs=out_specs, check_vma=False)
```

```python
import math

import jax
import jax.numpy as jnp
from jax import lax
from jax.sharding import Mesh, PartitionSpec as P

QH = 64
KVH = 8
HD = 64
FF = 2880
WINDOW = 128
R = 16
TENSOR = ("tz", "tx")


NORM_EPS = 1e-05
ROPE_BASE = 150000.0
SWIGLU_ALPHA = 1.702


def token_tables(length_row, adapter_row, first_row, row_count):
    prompt_ends = jnp.cumsum(length_row)
    prompt_starts = prompt_ends - length_row
    token_index = first_row + jnp.arange(row_count, dtype=jnp.int32)
    member = (token_index[:, None] >= prompt_starts[None, :]) & (
        token_index[:, None] < prompt_ends[None, :]
    )
    prompt_index = jnp.arange(length_row.shape[0], dtype=jnp.int32)
    segment = jnp.sum(jnp.where(member, prompt_index[None, :], 0), axis=1)
    prompt_begin = jnp.sum(jnp.where(member, prompt_starts[None, :], 0), axis=1)
    adapter = jnp.sum(jnp.where(member, adapter_row[None, :], 0), axis=1)
    return (segment, token_index - prompt_begin, adapter)


def rms_scale(row_block, gain):
    wide = row_block.astype(jnp.float32)
    mean_square = jnp.mean(wide * wide, axis=-1, keepdims=True)
    return (wide * lax.rsqrt(mean_square + NORM_EPS) * gain).astype(jnp.bfloat16)


def rotate(head_rows, position):
    half_width = head_rows.shape[-1] // 2
    freqs = jnp.exp(-math.log(ROPE_BASE) * jnp.arange(half_width, dtype=jnp.float32) / half_width)
    angles = position.astype(jnp.float32)[:, None] * freqs[None, :]
    cosine = jnp.cos(angles)[:, None, :]
    sine_val = jnp.sin(angles)[:, None, :]
    first_half = head_rows[..., :half_width]
    second_half = head_rows[..., half_width:]
    return jnp.concatenate(
        [
            first_half * cosine - second_half * sine_val,
            second_half * cosine + first_half * sine_val,
        ],
        axis=-1,
    )


def spread_rank(onehot, rank_rows):
    return (onehot[:, :, None] * rank_rows[:, None, :]).reshape(rank_rows.shape[0], -1)


def attend(queries, key_rows, value_rows, segment, sink_logits):
    row_count = queries.shape[0]
    block_rows = min(512, row_count)
    key_pad = jnp.pad(key_rows, ((WINDOW, 0), (0, 0), (0, 0)))
    value_pad = jnp.pad(value_rows, ((WINDOW, 0), (0, 0), (0, 0)))
    segment_pad = jnp.pad(segment, (WINDOW, 0), constant_values=-1)
    sink_weight = jnp.exp(sink_logits)[:, None]
    score_scale = queries.shape[-1] ** (-0.5)

    def one_block(block_start):
        row_pos = jnp.arange(block_rows, dtype=jnp.int32)[:, None] + WINDOW
        col_pos = jnp.arange(block_rows + WINDOW, dtype=jnp.int32)[None, :]
        allowed = (
            (segment[:, None] == segment_pad[None, :])
            & (col_pos <= row_pos)
            & (row_pos - col_pos < WINDOW)
        )
        scores = (
            jnp.einsum("qhd,khd->hqk", queries, key_pad, preferred_element_type=jnp.float32)
            * score_scale
        )
        weights = jnp.where(allowed[None], jnp.exp(scores), 0.0)
        denominator = sink_weight + jnp.sum(weights, axis=-1)
        weights_bf = (weights / denominator[..., None]).astype(jnp.bfloat16)
        mixed_block = jnp.einsum(
            "hqk,khd->qhd", weights_bf, value_pad, preferred_element_type=jnp.float32
        )
        return mixed_block.astype(jnp.bfloat16).reshape(block_rows, -1)

    block_starts = jnp.arange(row_count // block_rows, dtype=jnp.int32) * block_rows
    return lax.map(one_block, block_starts).reshape(row_count, -1)


def tensor_index():
    return lax.axis_index("tz") * lax.axis_size("tx") + lax.axis_index("tx")


def tensor_size():
    return lax.axis_size("tz") * lax.axis_size("tx")


def gather_tensor(block, axis=0):
    inner = lax.all_gather(block, "tx", axis=axis, tiled=True)
    return lax.all_gather(inner, "tz", axis=axis, tiled=True)


def scatter_tensor(block):
    inner = lax.psum_scatter(block, "tz", scatter_dimension=0, tiled=True)
    return lax.psum_scatter(inner, "tx", scatter_dimension=0, tiled=True)


def swap_owner(outgoing):
    return lax.all_to_all(outgoing, "adapter", split_axis=0, concat_axis=0, tiled=True)


def gather_tokens(row_block):
    return gather_tensor(row_block)


def tensor_total(partial_value):
    inner = lax.psum_scatter(partial_value.astype(jnp.bfloat16), "tz", scatter_dimension=0, tiled=True)
    inner = lax.psum(inner, "tx")
    return lax.all_gather(inner, "tz", axis=0, tiled=True).astype(jnp.float32)


def small_total(partial_value):
    inner = lax.psum(partial_value.astype(jnp.bfloat16), "tx")
    return lax.psum(inner, "tz").astype(jnp.float32)


def partial_sum(term_maker, own_rows):
    return scatter_tensor(
        term_maker(jnp.int32(0), tensor_size() * own_rows).astype(jnp.bfloat16)
    ).astype(jnp.float32)


def ask_owners(normed_own, bank, lengths, prompt_adapter, adapter_slot):
    own_rows = normed_own.shape[0]
    owner_count = lax.axis_size("adapter")
    owner_here = lax.axis_index("adapter")
    first_row = tensor_index() * own_rows
    stored, rank_width, width_d = bank.shape
    adapter_count = adapter_slot.shape[0]
    adapter_ids = jnp.arange(adapter_count, dtype=jnp.int32)

    def slots_of(length_row, adapter_row):
        adapter = token_tables(length_row, adapter_row, first_row, own_rows)[2]
        return jnp.sum(
            jnp.where(adapter[:, None] == adapter_ids[None, :], adapter_slot[None, :], 0), axis=1
        )

    all_slots = jax.vmap(slots_of)(lengths, prompt_adapter)
    own_slots = lax.dynamic_index_in_dim(all_slots, owner_here, 0, keepdims=False)
    route_mask = (own_slots // stored)[None, :] == jnp.arange(owner_count, dtype=jnp.int32)[:, None]
    outgoing = jnp.where(
        route_mask[:, :, None], normed_own[None, :, :], jnp.zeros((), jnp.bfloat16)
    )
    incoming = swap_owner(outgoing)
    local_slot = all_slots - owner_here * stored
    pick_hot = (
        local_slot[:, :, None] == jnp.arange(stored, dtype=jnp.int32)[None, None, :]
    ).astype(jnp.float32)
    flat_rows = incoming.reshape(owner_count * own_rows, width_d)
    projected = lax.dot_general(
        flat_rows,
        bank.reshape(stored * rank_width, width_d),
        (((1,), (1,)), ((), ())),
        preferred_element_type=jnp.float32,
    )
    projected = projected.reshape(owner_count, own_rows, stored, rank_width)
    answer = jnp.sum(projected * pick_hot[..., None], axis=2).astype(jnp.bfloat16)
    returned = swap_owner(answer.reshape(owner_count, own_rows * rank_width))
    return jnp.sum(
        returned.reshape(owner_count, own_rows, rank_width).astype(jnp.float32), axis=0
    ).astype(jnp.bfloat16)


def layer(
    tokens,
    gain_attention,
    query_weight,
    keyval_weight,
    output_weight,
    sink_logits,
    heads_down,
    query_up,
    keyval_up,
    output_down,
    output_up,
    gain_mixture,
    gate_up_weight,
    down_weight,
    mixture_down,
    mixture_up,
    lengths,
    prompt_adapter,
    adapter_slot,
    expert_ids,
    expert_weights,
):
    own_rows = tokens.shape[0]
    tensor_here = tensor_index()
    group_here = lax.axis_index("adapter")
    group_rows = own_rows * tensor_size()
    adapter_count = adapter_slot.shape[0]
    query_cols = query_weight.shape[1]
    local_count = output_up.shape[0]
    slice_width = down_weight.shape[0]
    first_own = tensor_here * own_rows
    entries_here = keyval_weight.shape[2]
    length_row = lax.dynamic_index_in_dim(lengths, group_here, 0, keepdims=False)
    adapter_row = lax.dynamic_index_in_dim(prompt_adapter, group_here, 0, keepdims=False)
    segment, position, adapter = token_tables(length_row, adapter_row, jnp.int32(0), group_rows)
    adapter_hit = adapter[:, None] == jnp.arange(adapter_count, dtype=jnp.int32)[None, :]
    onehot = adapter_hit.astype(jnp.bfloat16)
    local_ids = tensor_here * local_count + jnp.arange(local_count, dtype=jnp.int32)
    local_hot = (adapter[:, None] == local_ids[None, :]).astype(jnp.bfloat16)
    normed_own = rms_scale(tokens, gain_attention)
    tokens_all = gather_tokens(tokens)
    normed = rms_scale(tokens_all, gain_attention)
    rank_own = ask_owners(normed_own, heads_down, lengths, prompt_adapter, adapter_slot)
    rank_qkv = gather_tokens(rank_own)
    queries = jnp.dot(normed, query_weight, preferred_element_type=jnp.float32)
    queries = queries + jnp.dot(
        spread_rank(onehot, rank_qkv[:, :R]),
        query_up.reshape(adapter_count * R, query_cols),
        preferred_element_type=jnp.float32,
    )
    queries = rotate(queries.reshape(group_rows, query_cols // HD, HD), position).astype(
        jnp.bfloat16
    )
    heads_here = query_cols // HD
    tensor_count = tensor_size()
    dest_head = (jnp.arange(tensor_count, dtype=jnp.int32) * heads_here) // (QH // KVH)
    weight_send = jnp.moveaxis(jnp.take(keyval_weight, dest_head, axis=3), 3, 0)
    weight_recv = lax.all_to_all(weight_send, TENSOR, 0, 0, tiled=True)
    head_weight = jnp.transpose(weight_recv, (1, 2, 0, 3)).reshape(
        keyval_weight.shape[0], 2, tensor_count * entries_here
    )
    up_send = jnp.moveaxis(jnp.take(keyval_up, dest_head, axis=4), 4, 0)
    up_recv = lax.all_to_all(up_send, TENSOR, 0, 0, tiled=True)
    head_up = jnp.transpose(up_recv, (1, 2, 3, 0, 4)).reshape(
        adapter_count, 2, R, tensor_count * entries_here
    )
    key_part = jnp.dot(normed, head_weight[:, 0], preferred_element_type=jnp.float32)
    key_part = key_part + jnp.dot(
        spread_rank(onehot, rank_qkv[:, R : 2 * R]),
        head_up[:, 0].reshape(adapter_count * R, -1),
        preferred_element_type=jnp.float32,
    )
    value_part = jnp.dot(normed, head_weight[:, 1], preferred_element_type=jnp.float32)
    value_part = value_part + jnp.dot(
        spread_rank(onehot, rank_qkv[:, 2 * R : 3 * R]),
        head_up[:, 1].reshape(adapter_count * R, -1),
        preferred_element_type=jnp.float32,
    )
    key_rows = rotate(
        key_part.astype(jnp.bfloat16).astype(jnp.float32)[:, None, :], position
    ).astype(jnp.bfloat16)
    value_rows = value_part.astype(jnp.bfloat16)[:, None, :]
    mixed_rows = attend(
        queries,
        jnp.broadcast_to(key_rows, (group_rows, heads_here, HD)),
        jnp.broadcast_to(value_rows, (group_rows, heads_here, HD)),
        segment,
        sink_logits,
    )
    prompt_count = adapter_row.shape[0]
    owner_count = lax.axis_size("adapter")
    bank_send = jnp.broadcast_to(mixture_down[None], (owner_count,) + mixture_down.shape)
    bank_all = lax.all_to_all(bank_send, "adapter", 0, 0, tiled=True)
    bank_all = bank_all.reshape(-1, R, mixture_down.shape[-1])
    rank_table = output_down.reshape(adapter_count * R, query_cols)
    rank_terms = lax.dot_general(
        mixed_rows, rank_table, (((1,), (1,)), ((), ())), preferred_element_type=jnp.float32
    )
    rank_terms = jnp.sum(
        rank_terms.reshape(group_rows, adapter_count, R) * onehot[:, :, None], axis=1
    )
    rank_out = small_total(rank_terms).astype(jnp.bfloat16)
    spread_out = spread_rank(local_hot, rank_out)
    up_out = output_up.reshape(local_count * R, -1)
    term = jnp.dot(mixed_rows, output_weight, preferred_element_type=jnp.float32)
    attn_all = tensor_total(
        term + jnp.dot(spread_out, up_out, preferred_element_type=jnp.float32)
    )
    hidden_all = tokens_all.astype(jnp.float32) + attn_all
    normed_two = rms_scale(hidden_all, gain_mixture)
    hidden_own = lax.dynamic_slice_in_dim(hidden_all, first_own, own_rows, 0)
    normed_two_own = lax.dynamic_slice_in_dim(normed_two, first_own, own_rows, 0)
    bank_group = jnp.take(bank_all, jnp.take(adapter_slot, adapter_row), axis=0)
    moe_proj = lax.dot_general(
        normed_two,
        bank_group.reshape(prompt_count * R, -1),
        (((1,), (1,)), ((), ())),
        preferred_element_type=jnp.float32,
    )
    segment_hot = (segment[:, None] == jnp.arange(prompt_count, dtype=jnp.int32)[None, :]).astype(
        jnp.float32
    )
    rank_moe = jnp.sum(
        moe_proj.reshape(group_rows, prompt_count, R) * segment_hot[:, :, None], axis=1
    ).astype(jnp.bfloat16)
    expert_here = tensor_here * slice_width // FF
    named = expert_ids == expert_here
    route_weight = jnp.sum(jnp.where(named, expert_weights, 0.0), axis=1)
    picked = jnp.any(named, axis=1)
    gate_val = jnp.dot(normed_two, gate_up_weight[:, 0], preferred_element_type=jnp.float32)
    lift_val = jnp.dot(normed_two, gate_up_weight[:, 1], preferred_element_type=jnp.float32)
    active = (
        (lift_val + 1.0)
        * gate_val
        * jax.nn.sigmoid(SWIGLU_ALPHA * gate_val)
        * route_weight[:, None]
    ).astype(jnp.bfloat16)
    expert_terms = jnp.dot(active, down_weight, preferred_element_type=jnp.float32)
    spread_moe = spread_rank(local_hot, rank_moe)
    up_moe = mixture_up.reshape(local_count * R, -1)

    def moe_term(row_start, row_count):
        expert_rows = jnp.where(picked[:, None], expert_terms, 0.0)
        return expert_rows + jnp.dot(spread_moe, up_moe, preferred_element_type=jnp.float32)

    moe_own = partial_sum(moe_term, own_rows)
    return (hidden_own + moe_own).astype(jnp.bfloat16)


def split_mesh(mesh):
    grid = mesh.devices
    tensor_count, adapter_count = grid.shape
    x_coords = {getattr(d, "coords", (i,))[0] for i, d in enumerate(grid[:, 0])}
    x_count = len(x_coords) if tensor_count % len(x_coords) == 0 else 1
    return Mesh(grid.reshape(tensor_count // x_count, x_count, adapter_count), ("tz", "tx", "adapter"))


def solution(mesh):
    mesh = split_mesh(mesh)
    in_specs = (
        P(("adapter", "tz", "tx"), None),
        P(),
        P(None, TENSOR),
        P(None, None, TENSOR, None),
        P(TENSOR, None),
        P(TENSOR),
        P("adapter", None, None),
        P(None, None, TENSOR),
        P(None, None, None, TENSOR, None),
        P(None, None, TENSOR),
        P(TENSOR, None, None),
        P(),
        P(None, None, TENSOR),
        P(TENSOR, None),
        P("adapter", None, None),
        P(TENSOR, None, None),
        P(),
        P(),
        P(),
        P("adapter", None),
        P("adapter", None),
    )
    out_specs = P(("adapter", "tz", "tx"), None)
    return jax.shard_map(layer, mesh=mesh, in_specs=in_specs, out_specs=out_specs, check_vma=False)
```

```python
import math

import jax
import jax.numpy as jnp
from jax import lax
from jax.sharding import Mesh, PartitionSpec as P

QH = 64
KVH = 8
HD = 64
FF = 2880
WINDOW = 128
R = 16
TENSOR = ("tz", "tx")


NORM_EPS = 1e-05
ROPE_BASE = 150000.0
SWIGLU_ALPHA = 1.702


def token_tables(length_row, adapter_row, first_row, row_count):
    prompt_ends = jnp.cumsum(length_row)
    prompt_starts = prompt_ends - length_row
    token_index = first_row + jnp.arange(row_count, dtype=jnp.int32)
    member = (token_index[:, None] >= prompt_starts[None, :]) & (
        token_index[:, None] < prompt_ends[None, :]
    )
    prompt_index = jnp.arange(length_row.shape[0], dtype=jnp.int32)
    segment = jnp.sum(jnp.where(member, prompt_index[None, :], 0), axis=1)
    prompt_begin = jnp.sum(jnp.where(member, prompt_starts[None, :], 0), axis=1)
    adapter = jnp.sum(jnp.where(member, adapter_row[None, :], 0), axis=1)
    return (segment, token_index - prompt_begin, adapter)


def settle(values):
    return lax.optimization_barrier(values.astype(jnp.bfloat16)).astype(jnp.float32)


def rms_scale(row_block, gain):
    wide = row_block.astype(jnp.float32)
    mean_square = jnp.mean(wide * wide, axis=-1, keepdims=True)
    return (wide * lax.rsqrt(mean_square + NORM_EPS) * gain).astype(jnp.bfloat16)


def rotate(head_rows, position):
    half_width = head_rows.shape[-1] // 2
    freqs = jnp.exp(-math.log(ROPE_BASE) * jnp.arange(half_width, dtype=jnp.float32) / half_width)
    angles = position.astype(jnp.float32)[:, None] * freqs[None, :]
    cosine = jnp.cos(angles)[:, None, :]
    sine_val = jnp.sin(angles)[:, None, :]
    first_half = head_rows[..., :half_width]
    second_half = head_rows[..., half_width:]
    return jnp.concatenate(
        [
            first_half * cosine - second_half * sine_val,
            second_half * cosine + first_half * sine_val,
        ],
        axis=-1,
    )


def spread_rank(onehot, rank_rows):
    return (onehot[:, :, None] * rank_rows[:, None, :]).reshape(rank_rows.shape[0], -1)


def attend(queries, key_rows, value_rows, segment, sink_logits):
    row_count = queries.shape[0]
    block_rows = min(512, row_count)
    key_pad = jnp.pad(key_rows, ((WINDOW, 0), (0, 0), (0, 0)))
    value_pad = jnp.pad(value_rows, ((WINDOW, 0), (0, 0), (0, 0)))
    segment_pad = jnp.pad(segment, (WINDOW, 0), constant_values=-1)
    sink_weight = jnp.exp(sink_logits)[:, None]
    score_scale = queries.shape[-1] ** (-0.5)

    def one_block(block_start):
        row_pos = jnp.arange(block_rows, dtype=jnp.int32)[:, None] + WINDOW
        col_pos = jnp.arange(block_rows + WINDOW, dtype=jnp.int32)[None, :]
        allowed = (
            (segment[:, None] == segment_pad[None, :])
            & (col_pos <= row_pos)
            & (row_pos - col_pos < WINDOW)
        )
        scores = (
            jnp.einsum("qhd,khd->hqk", queries, key_pad, preferred_element_type=jnp.float32)
            * score_scale
        )
        weights = jnp.where(allowed[None], jnp.exp(scores), 0.0)
        denominator = sink_weight + jnp.sum(weights, axis=-1)
        weights_bf = (weights / denominator[..., None]).astype(jnp.bfloat16)
        mixed_block = jnp.einsum(
            "hqk,khd->qhd", weights_bf, value_pad, preferred_element_type=jnp.float32
        )
        return mixed_block.astype(jnp.bfloat16).reshape(block_rows, -1)

    block_starts = jnp.arange(row_count // block_rows, dtype=jnp.int32) * block_rows
    return lax.map(one_block, block_starts).reshape(row_count, -1)


def tensor_index():
    return lax.axis_index("tz") * lax.axis_size("tx") + lax.axis_index("tx")


def tensor_size():
    return lax.axis_size("tz") * lax.axis_size("tx")


def gather_tensor(block, axis=0):
    inner = lax.all_gather(block, "tx", axis=axis, tiled=True)
    return lax.all_gather(inner, "tz", axis=axis, tiled=True)


def scatter_tensor(block):
    inner = lax.psum_scatter(block, "tz", scatter_dimension=0, tiled=True)
    return lax.psum_scatter(inner, "tx", scatter_dimension=0, tiled=True)


def swap_owner(outgoing):
    return lax.all_to_all(outgoing, "adapter", split_axis=0, concat_axis=0, tiled=True)


def gather_tokens(row_block):
    return gather_tensor(row_block)


def tensor_total(partial_value):
    return gather_tensor(scatter_tensor(partial_value.astype(jnp.bfloat16))).astype(jnp.float32)


def small_total(partial_value):
    inner = lax.psum(partial_value.astype(jnp.bfloat16), "tz")
    return lax.psum(inner, "tx").astype(jnp.float32)


def partial_sum(term_maker, own_rows):
    return scatter_tensor(
        term_maker(jnp.int32(0), tensor_size() * own_rows).astype(jnp.bfloat16)
    ).astype(jnp.float32)


def ask_owners(normed_own, bank, lengths, prompt_adapter, adapter_slot):
    own_rows = normed_own.shape[0]
    owner_count = lax.axis_size("adapter")
    owner_here = lax.axis_index("adapter")
    first_row = tensor_index() * own_rows
    stored, rank_width, width_d = bank.shape
    adapter_count = adapter_slot.shape[0]
    adapter_ids = jnp.arange(adapter_count, dtype=jnp.int32)

    def slots_of(length_row, adapter_row):
        adapter = token_tables(length_row, adapter_row, first_row, own_rows)[2]
        return jnp.sum(
            jnp.where(adapter[:, None] == adapter_ids[None, :], adapter_slot[None, :], 0), axis=1
        )

    all_slots = jax.vmap(slots_of)(lengths, prompt_adapter)
    own_slots = lax.dynamic_index_in_dim(all_slots, owner_here, 0, keepdims=False)
    route_mask = (own_slots // stored)[None, :] == jnp.arange(owner_count, dtype=jnp.int32)[:, None]
    outgoing = jnp.where(
        route_mask[:, :, None], normed_own[None, :, :], jnp.zeros((), jnp.bfloat16)
    )
    incoming = swap_owner(outgoing)
    local_slot = all_slots - owner_here * stored
    pick_hot = (
        local_slot[:, :, None] == jnp.arange(stored, dtype=jnp.int32)[None, None, :]
    ).astype(jnp.float32)
    flat_rows = incoming.reshape(owner_count * own_rows, width_d)
    projected = lax.dot_general(
        flat_rows,
        bank.reshape(stored * rank_width, width_d),
        (((1,), (1,)), ((), ())),
        preferred_element_type=jnp.float32,
    )
    projected = projected.reshape(owner_count, own_rows, stored, rank_width)
    answer = jnp.sum(projected * pick_hot[..., None], axis=2).astype(jnp.bfloat16)
    returned = swap_owner(answer.reshape(owner_count, own_rows * rank_width))
    return jnp.sum(
        returned.reshape(owner_count, own_rows, rank_width).astype(jnp.float32), axis=0
    ).astype(jnp.bfloat16)


def layer(
    tokens,
    gain_attention,
    query_weight,
    keyval_weight,
    output_weight,
    sink_logits,
    heads_down,
    query_up,
    keyval_up,
    output_down,
    output_up,
    gain_mixture,
    gate_up_weight,
    down_weight,
    mixture_down,
    mixture_up,
    lengths,
    prompt_adapter,
    adapter_slot,
    expert_ids,
    expert_weights,
):
    own_rows = tokens.shape[0]
    tensor_here = tensor_index()
    group_here = lax.axis_index("adapter")
    group_rows = own_rows * tensor_size()
    adapter_count = adapter_slot.shape[0]
    query_cols = query_weight.shape[1]
    local_count = output_up.shape[0]
    slice_width = down_weight.shape[0]
    first_own = tensor_here * own_rows
    entries_here = keyval_weight.shape[2]
    length_row = lax.dynamic_index_in_dim(lengths, group_here, 0, keepdims=False)
    adapter_row = lax.dynamic_index_in_dim(prompt_adapter, group_here, 0, keepdims=False)
    segment, position, adapter = token_tables(length_row, adapter_row, jnp.int32(0), group_rows)
    adapter_hit = adapter[:, None] == jnp.arange(adapter_count, dtype=jnp.int32)[None, :]
    onehot = adapter_hit.astype(jnp.bfloat16)
    local_ids = tensor_here * local_count + jnp.arange(local_count, dtype=jnp.int32)
    local_hot = (adapter[:, None] == local_ids[None, :]).astype(jnp.bfloat16)
    normed_own = rms_scale(tokens, gain_attention)
    tokens_all = gather_tokens(tokens)
    normed = rms_scale(tokens_all, gain_attention)
    rank_own = ask_owners(normed_own, heads_down, lengths, prompt_adapter, adapter_slot)
    rank_qkv = gather_tokens(rank_own)
    queries = jnp.dot(normed, query_weight, preferred_element_type=jnp.float32)
    queries = queries + jnp.dot(
        spread_rank(onehot, rank_qkv[:, :R]),
        query_up.reshape(adapter_count * R, query_cols),
        preferred_element_type=jnp.float32,
    )
    queries = rotate(queries.reshape(group_rows, query_cols // HD, HD), position).astype(
        jnp.bfloat16
    )
    heads_here = query_cols // HD
    tensor_count = tensor_size()
    dest_head = (jnp.arange(tensor_count, dtype=jnp.int32) * heads_here) // (QH // KVH)
    weight_send = jnp.moveaxis(jnp.take(keyval_weight, dest_head, axis=3), 3, 0)
    weight_recv = lax.all_to_all(weight_send, TENSOR, 0, 0, tiled=True)
    head_weight = jnp.transpose(weight_recv, (1, 2, 0, 3)).reshape(
        keyval_weight.shape[0], 2, tensor_count * entries_here
    )
    up_send = jnp.moveaxis(jnp.take(keyval_up, dest_head, axis=4), 4, 0)
    up_recv = lax.all_to_all(up_send, TENSOR, 0, 0, tiled=True)
    head_up = jnp.transpose(up_recv, (1, 2, 3, 0, 4)).reshape(
        adapter_count, 2, R, tensor_count * entries_here
    )
    key_part = jnp.dot(normed, head_weight[:, 0], preferred_element_type=jnp.float32)
    key_part = key_part + jnp.dot(
        spread_rank(onehot, rank_qkv[:, R : 2 * R]),
        head_up[:, 0].reshape(adapter_count * R, -1),
        preferred_element_type=jnp.float32,
    )
    value_part = jnp.dot(normed, head_weight[:, 1], preferred_element_type=jnp.float32)
    value_part = value_part + jnp.dot(
        spread_rank(onehot, rank_qkv[:, 2 * R : 3 * R]),
        head_up[:, 1].reshape(adapter_count * R, -1),
        preferred_element_type=jnp.float32,
    )
    key_rows = rotate(
        key_part.astype(jnp.bfloat16).astype(jnp.float32)[:, None, :], position
    ).astype(jnp.bfloat16)
    value_rows = value_part.astype(jnp.bfloat16)[:, None, :]
    mixed_rows = attend(
        queries,
        jnp.broadcast_to(key_rows, (group_rows, heads_here, HD)),
        jnp.broadcast_to(value_rows, (group_rows, heads_here, HD)),
        segment,
        sink_logits,
    )
    prompt_count = adapter_row.shape[0]
    owner_count = lax.axis_size("adapter")
    bank_send = jnp.broadcast_to(mixture_down[None], (owner_count,) + mixture_down.shape)
    bank_all = lax.all_to_all(bank_send, "adapter", 0, 0, tiled=True)
    bank_all = bank_all.reshape(-1, R, mixture_down.shape[-1])
    rank_table = output_down.reshape(adapter_count * R, query_cols)
    rank_terms = lax.dot_general(
        mixed_rows, rank_table, (((1,), (1,)), ((), ())), preferred_element_type=jnp.float32
    )
    rank_terms = jnp.sum(
        rank_terms.reshape(group_rows, adapter_count, R) * onehot[:, :, None], axis=1
    )
    rank_out = small_total(settle(rank_terms)).astype(jnp.bfloat16)
    spread_out = spread_rank(local_hot, rank_out)
    up_out = output_up.reshape(local_count * R, -1)
    term = jnp.dot(mixed_rows, output_weight, preferred_element_type=jnp.float32)
    attn_all = tensor_total(
        term + jnp.dot(spread_out, up_out, preferred_element_type=jnp.float32)
    )
    hidden_all = tokens_all.astype(jnp.float32) + attn_all
    normed_two = rms_scale(hidden_all, gain_mixture)
    hidden_own = lax.dynamic_slice_in_dim(hidden_all, first_own, own_rows, 0)
    normed_two_own = lax.dynamic_slice_in_dim(normed_two, first_own, own_rows, 0)
    bank_group = jnp.take(bank_all, jnp.take(adapter_slot, adapter_row), axis=0)
    moe_proj = lax.dot_general(
        normed_two,
        bank_group.reshape(prompt_count * R, -1),
        (((1,), (1,)), ((), ())),
        preferred_element_type=jnp.float32,
    )
    segment_hot = (segment[:, None] == jnp.arange(prompt_count, dtype=jnp.int32)[None, :]).astype(
        jnp.float32
    )
    rank_moe = jnp.sum(
        moe_proj.reshape(group_rows, prompt_count, R) * segment_hot[:, :, None], axis=1
    ).astype(jnp.bfloat16)
    expert_here = tensor_here * slice_width // FF
    named = expert_ids == expert_here
    route_weight = jnp.sum(jnp.where(named, expert_weights, 0.0), axis=1)
    picked = jnp.any(named, axis=1)
    gate_val = jnp.dot(normed_two, gate_up_weight[:, 0], preferred_element_type=jnp.float32)
    lift_val = jnp.dot(normed_two, gate_up_weight[:, 1], preferred_element_type=jnp.float32)
    active = (
        (lift_val + 1.0)
        * gate_val
        * jax.nn.sigmoid(SWIGLU_ALPHA * gate_val)
        * route_weight[:, None]
    ).astype(jnp.bfloat16)
    expert_terms = jnp.dot(active, down_weight, preferred_element_type=jnp.float32)
    spread_moe = spread_rank(local_hot, rank_moe)
    up_moe = mixture_up.reshape(local_count * R, -1)

    def moe_term(row_start, row_count):
        expert_rows = jnp.where(picked[:, None], expert_terms, 0.0)
        return expert_rows + jnp.dot(spread_moe, up_moe, preferred_element_type=jnp.float32)

    moe_own = partial_sum(moe_term, own_rows)
    return (hidden_own + moe_own).astype(jnp.bfloat16)


def split_mesh(mesh):
    grid = mesh.devices
    tensor_count, adapter_count = grid.shape
    x_coords = {getattr(d, "coords", (i,))[0] for i, d in enumerate(grid[:, 0])}
    x_count = len(x_coords) if tensor_count % len(x_coords) == 0 else 1
    return Mesh(grid.reshape(tensor_count // x_count, x_count, adapter_count), ("tz", "tx", "adapter"))


def solution(mesh):
    mesh = split_mesh(mesh)
    in_specs = (
        P(("adapter", "tz", "tx"), None),
        P(),
        P(None, TENSOR),
        P(None, None, TENSOR, None),
        P(TENSOR, None),
        P(TENSOR),
        P("adapter", None, None),
        P(None, None, TENSOR),
        P(None, None, None, TENSOR, None),
        P(None, None, TENSOR),
        P(TENSOR, None, None),
        P(),
        P(None, None, TENSOR),
        P(TENSOR, None),
        P("adapter", None, None),
        P(TENSOR, None, None),
        P(),
        P(),
        P(),
        P("adapter", None),
        P("adapter", None),
    )
    out_specs = P(("adapter", "tz", "tx"), None)
    return jax.shard_map(layer, mesh=mesh, in_specs=in_specs, out_specs=out_specs, check_vma=False)
```
